128 devices in a mesh: wave: 32 (over x, z, core), dof: 4 (over y).
Axes of the slice: x: 4, y: 4, z: 4, core: 2. Of those that a mesh axis runs over, the one named last changes fastest.
Arguments:
- green: bfloat16 [2, 2048, 512, 512], P(None, 'wave', None, 'dof'), may hold values from -0.25 to 0.25
- rough: float32 [2, 2048, 512], P(None, 'wave'), may hold values from -6 to 6
- axle_pos: int32 [128, 32], replicated, may hold values from 0 to 2047
- axle_load: float32 [128, 32], replicated, may hold values from 0.5 to 1.5
- rows: int32 [1024, 16], replicated, may hold values from 0 to 2047
- counts: int32 [1024], replicated, may hold values from 1 to 16, as said below
- coupling: bfloat16 [1024, 512], P(None, 'dof'), may hold values from -0.25 to 0.25
Outputs:
- response: float32 [1024, 128], P('dof', 'wave')
The draws below stay inside these ranges and needn't reach their ends.
Inputs may be any that keep to these rules, and one draw needn't show every extreme that they name: Building b uses its first counts[b] stations; some building uses all 16.
All inputs are finite; a program needn't handle non-finite values.
Results may differ from the reference program's by a relative error of at most 0.005.
Values may be sent and summed in bfloat16 or wider, within the bound.
A program may use at most 320 MiB of HBM per device.

```python
import math
import jax
import jax.numpy as jnp
from jax import lax

K = 2048
NDOF = 512
NC = 128
AXLES = 32
NB = 1024
RMAX = 16


def draw_counts(key, part):
    first_key, second_key = jax.random.split(jax.random.fold_in(key, 17))
    values = jax.random.randint(first_key, (NB,), 1, RMAX + 1)
    chosen = jax.random.randint(second_key, (), 0, NB)
    return values.at[chosen].set(RMAX).astype(jnp.int32)


def plant(values, key, low, high):
    dims = values.shape
    place = [jax.random.randint(jax.random.fold_in(key, axis), (), 0, dims[axis]) for axis in range(len(dims))]
    values = values.at[tuple(place)].set(low)
    longest = dims.index(max(dims))
    place[longest] = (place[longest] + 1) % dims[longest]
    return values.at[tuple(place)].set(high)


def steps_of(key, shape, pieces, smallest, top_value):
    def one(dim, shards_of):
        draws = jax.random.uniform(jax.random.fold_in(jax.random.fold_in(key, 6), dim), (shards_of,), jnp.float32, smallest / len(pieces), top_value / len(pieces))
        return jnp.repeat(jnp.exp(draws), shape[dim] // shards_of).reshape((-1,) + (1,) * (len(shape) - dim - 1))

    loudness = one(*pieces[0])
    for cut in pieces[1:]:
        loudness = loudness * one(*cut)
    return loudness


def noise(own_key, shape, width, reach, pieces=(), held_as=jnp.bfloat16):
    level = steps_of(own_key, shape, pieces, -0.22, 0.18) if pieces else 1.0
    array = jax.random.normal(own_key, shape, jnp.float32) * width * level
    return jnp.minimum(jnp.maximum(array, -reach), reach).astype(held_as)


def setup_inputs(seed: int = 0) -> dict:
    seeds = jax.random.split(jax.random.key(seed), 8)
    return {
        "green": noise(seeds[0], (2, K, NDOF, NDOF), NDOF ** -0.5, 0.25, ((1, 32), (3, 4))),
        "rough": noise(seeds[1], (2, K, NDOF), 1.0, 6.0, ((1, 32),), jnp.float32),
        "axle_pos": plant(jax.random.randint(seeds[2], (NC, AXLES), 0, K), jax.random.fold_in(seeds[2], 1), 0, K - 1).astype(jnp.int32),
        "axle_load": jnp.clip(jax.random.uniform(seeds[3], (NC, AXLES), jnp.float32, 0.5, 1.5), 0.5, 1.5),
        "rows": plant(jax.random.randint(seeds[4], (NB, RMAX), 0, K), jax.random.fold_in(seeds[4], 1), 0, K - 1).astype(jnp.int32),
        "counts": draw_counts(jax.random.fold_in(seeds[7], 71), 0),
        "coupling": noise(seeds[6], (NB, NDOF), NDOF ** -0.5, 0.25, ((1, 4),)),
    }


def make_table():
    stations = jnp.arange(K, dtype=jnp.int32)
    product = stations[:, None] * stations[None, :] % K
    angle = product.astype(jnp.float32) * (2.0 * math.pi / K)
    scale = 1.0 / math.sqrt(K)
    table = jnp.stack([jnp.cos(angle) * scale, -jnp.sin(angle) * scale], axis=2)
    return table.reshape(K, 2 * K).astype(jnp.bfloat16)

def reference(green, rough, axle_pos, axle_load, rows, counts, coupling):
    waves = jnp.arange(K, dtype=jnp.int32)
    product = waves[:, None, None] * axle_pos[None, :, :] % K
    angle = product.astype(jnp.float32) * (2.0 * math.pi / K)
    norm_axle = 1.0 / math.sqrt(AXLES)
    phase_re = lax.optimization_barrier(jnp.sum(axle_load[None] * jnp.cos(angle), axis=2)) * norm_axle
    phase_im = -lax.optimization_barrier(jnp.sum(axle_load[None] * jnp.sin(angle), axis=2)) * norm_axle
    force_re = rough[0][:, :, None] * phase_re[:, None, :] - rough[1][:, :, None] * phase_im[:, None, :]
    force_im = rough[0][:, :, None] * phase_im[:, None, :] + rough[1][:, :, None] * phase_re[:, None, :]
    force = jnp.concatenate([force_re, force_im], axis=2).astype(jnp.bfloat16)
    case_count = axle_pos.shape[0]

    def one_wave(operands):
        green_one, force_one = operands
        prod_real = jnp.dot(green_one[0].T, force_one, preferred_element_type=jnp.float32)
        prod_imag = jnp.dot(green_one[1].T, force_one, preferred_element_type=jnp.float32)
        spec_re = prod_real[:, :case_count] - prod_imag[:, case_count:]
        spec_im = prod_real[:, case_count:] + prod_imag[:, :case_count]
        return jnp.stack([spec_re, spec_im], axis=0).astype(jnp.bfloat16)
    spectra = lax.map(one_wave, (jnp.transpose(green, (1, 0, 2, 3)), force))
    table = make_table()
    flat = spectra.reshape(K * 2, NDOF * case_count)
    field = jnp.dot(table, flat, preferred_element_type=jnp.float32)
    slots = (jnp.arange(RMAX, dtype=jnp.int32)[None, :] < counts[:, None]).astype(jnp.float32)
    building_ids = jnp.broadcast_to(jnp.arange(NB, dtype=jnp.int32)[:, None], (NB, RMAX))
    occupancy = jnp.zeros((NB, K), jnp.float32).at[building_ids, rows].add(slots).astype(jnp.bfloat16)
    gathered = jnp.dot(occupancy.astype(jnp.float32), field, precision=lax.Precision.HIGHEST, preferred_element_type=jnp.float32).reshape(NB, NDOF, case_count)
    summed = jnp.einsum('bi,bic->bc', coupling.astype(jnp.float32), gathered, precision=lax.Precision.HIGHEST)
    return summed / counts.astype(jnp.float32)[:, None]
```

```python
import math

import jax
import jax.numpy as jnp
from jax import lax
from jax.sharding import PartitionSpec as P

K = 2048


def split_bf16(x):
    hi = x.astype(jnp.bfloat16)
    lo = (x - hi.astype(jnp.float32)).astype(jnp.bfloat16)
    return hi, lo


def body(green, rough, axle_pos, axle_load, rows, counts, coupling):
    wave_count = green.shape[1]
    case_count = axle_pos.shape[0]
    building_count = rows.shape[0]
    slot_count = rows.shape[1]
    dof_size = lax.axis_size("dof")
    own_buildings = building_count // dof_size
    waves = lax.axis_index("wave") * wave_count + jnp.arange(wave_count, dtype=jnp.int32)

    product = waves[:, None, None] * axle_pos[None, :, :] % K
    angle = product.astype(jnp.float32) * (2.0 * math.pi / K)
    norm_axle = 1.0 / math.sqrt(axle_pos.shape[1])
    phase_re = jnp.sum(axle_load[None] * jnp.cos(angle), axis=2) * norm_axle
    phase_im = -jnp.sum(axle_load[None] * jnp.sin(angle), axis=2) * norm_axle

    re_hi, re_lo = split_bf16(rough[0])
    im_hi, im_lo = split_bf16(rough[1])
    lhs = jnp.stack([re_hi, re_lo, im_hi, im_lo], axis=1)
    prod = jnp.einsum("mkj,gmji->gmki", lhs, green, preferred_element_type=jnp.float32)
    gre_rre = prod[0, :, 0] + prod[0, :, 1]
    gre_rim = prod[0, :, 2] + prod[0, :, 3]
    gim_rre = prod[1, :, 0] + prod[1, :, 1]
    gim_rim = prod[1, :, 2] + prod[1, :, 3]
    h_cat = jnp.concatenate([gre_rre - gim_rim, gre_rim + gim_rre], axis=0)

    h_hi, h_lo = split_bf16(h_cat)
    rhs = jnp.concatenate([h_hi, h_lo], axis=0)
    both = jnp.einsum("bi,ni->bn", coupling, rhs, preferred_element_type=jnp.float32)
    v_part = both[:, : 2 * wave_count] + both[:, 2 * wave_count :]
    v_own = lax.psum_scatter(v_part, "dof", scatter_dimension=0, tiled=True)
    v_re = v_own[:, :wave_count]
    v_im = v_own[:, wave_count:]

    first = lax.axis_index("dof") * own_buildings
    rows_own = lax.dynamic_slice_in_dim(rows, first, own_buildings, 0)
    counts_own = lax.dynamic_slice_in_dim(counts, first, own_buildings, 0)
    used = (jnp.arange(slot_count, dtype=jnp.int32)[None, :] < counts_own[:, None]).astype(jnp.float32)
    station_prod = rows_own[:, :, None] * waves[None, None, :] % K
    station_angle = station_prod.astype(jnp.float32) * (2.0 * math.pi / K)
    scale = 1.0 / math.sqrt(K)
    t_re = (jnp.cos(station_angle) * scale).astype(jnp.bfloat16).astype(jnp.float32)
    t_im = (-jnp.sin(station_angle) * scale).astype(jnp.bfloat16).astype(jnp.float32)
    w_re = jnp.sum(used[:, :, None] * t_re, axis=1)
    w_im = jnp.sum(used[:, :, None] * t_im, axis=1)

    a_part = w_re * v_re + w_im * v_im
    b_part = w_im * v_re - w_re * v_im
    ab = jnp.concatenate([a_part, b_part], axis=1)
    phase_cat = jnp.concatenate([phase_re, phase_im], axis=0)
    partial = jnp.dot(
        phase_cat.T, ab.T, precision=lax.Precision.HIGHEST, preferred_element_type=jnp.float32
    )
    summed = lax.psum_scatter(partial, "wave", scatter_dimension=0, tiled=True)
    return summed.T / counts_own.astype(jnp.float32)[:, None]


def solution(mesh):
    in_specs = (
        P(None, "wave", None, "dof"),
        P(None, "wave", None),
        P(),
        P(),
        P(),
        P(),
        P(None, "dof"),
    )
    out_specs = P("dof", "wave")
    return jax.shard_map(body, mesh=mesh, in_specs=in_specs, out_specs=out_specs, check_vma=False)
```

```python
import math

import jax
import jax.numpy as jnp
from jax import lax
from jax.experimental import pallas as pl
from jax.experimental.pallas import tpu as pltpu
from jax.sharding import PartitionSpec as P

K = 2048


def split_bf16(x):
    hi = x.astype(jnp.bfloat16)
    lo = (x - hi.astype(jnp.float32)).astype(jnp.bfloat16)
    return hi, lo


def scatter_sum(x, axis, collective_id):
    n = x.shape[0]
    block = x.shape[1:]
    mesh_id = pl.DeviceIdType.MESH

    def kernel(x_ref, out_ref, recv, send_sems, recv_sems):
        me = lax.axis_index(axis)
        barrier = pltpu.get_barrier_semaphore()
        for k in range(1, n):
            peer = lax.rem(me + k, n)
            pl.semaphore_signal(barrier, inc=1, device_id={axis: peer}, device_id_type=mesh_id)
        pl.semaphore_wait(barrier, n - 1)
        copies = []
        for k in range(1, n):
            peer = lax.rem(me + k, n)
            copy = pltpu.make_async_remote_copy(
                src_ref=x_ref.at[peer],
                dst_ref=recv.at[k - 1],
                send_sem=send_sems.at[k - 1],
                recv_sem=recv_sems.at[k - 1],
                device_id={axis: peer},
                device_id_type=mesh_id,
            )
            copy.start()
            copies.append(copy)
        for copy in copies:
            copy.wait()
        total = x_ref[me]
        for k in range(n - 1):
            total = total + recv[k]
        out_ref[...] = total

    return pl.pallas_call(
        kernel,
        out_shape=jax.ShapeDtypeStruct(block, x.dtype),
        in_specs=[pl.BlockSpec(memory_space=pltpu.VMEM)],
        out_specs=pl.BlockSpec(memory_space=pltpu.VMEM),
        scratch_shapes=[
            pltpu.VMEM((n - 1,) + block, x.dtype),
            pltpu.SemaphoreType.DMA((n - 1,)),
            pltpu.SemaphoreType.DMA((n - 1,)),
        ],
        compiler_params=pltpu.CompilerParams(collective_id=collective_id, has_side_effects=True),
    )(x)


def body(green, rough, axle_pos, axle_load, rows, counts, coupling):
    wave_count = green.shape[1]
    case_count = axle_pos.shape[0]
    building_count = rows.shape[0]
    slot_count = rows.shape[1]
    dof_size = lax.axis_size("dof")
    own_buildings = building_count // dof_size
    waves = lax.axis_index("wave") * wave_count + jnp.arange(wave_count, dtype=jnp.int32)

    product = waves[:, None, None] * axle_pos[None, :, :] % K
    angle = product.astype(jnp.float32) * (2.0 * math.pi / K)
    norm_axle = 1.0 / math.sqrt(axle_pos.shape[1])
    phase_re = jnp.sum(axle_load[None] * jnp.cos(angle), axis=2) * norm_axle
    phase_im = -jnp.sum(axle_load[None] * jnp.sin(angle), axis=2) * norm_axle

    re_hi, re_lo = split_bf16(rough[0])
    im_hi, im_lo = split_bf16(rough[1])
    lhs = jnp.stack([re_hi, re_lo, im_hi, im_lo], axis=1)
    prod = jnp.einsum("mkj,gmji->gmki", lhs, green, preferred_element_type=jnp.float32)
    gre_rre = prod[0, :, 0] + prod[0, :, 1]
    gre_rim = prod[0, :, 2] + prod[0, :, 3]
    gim_rre = prod[1, :, 0] + prod[1, :, 1]
    gim_rim = prod[1, :, 2] + prod[1, :, 3]
    h_cat = jnp.concatenate([gre_rre - gim_rim, gre_rim + gim_rre], axis=0)

    h_hi, h_lo = split_bf16(h_cat)
    rhs = jnp.concatenate([h_hi, h_lo], axis=0)
    both = jnp.einsum("bi,ni->bn", coupling, rhs, preferred_element_type=jnp.float32)
    v_part = both[:, : 2 * wave_count] + both[:, 2 * wave_count :]
    v_own = scatter_sum(v_part.reshape(dof_size, own_buildings, 2 * wave_count), "dof", 0)
    v_re = v_own[:, :wave_count]
    v_im = v_own[:, wave_count:]

    first = lax.axis_index("dof") * own_buildings
    rows_own = lax.dynamic_slice_in_dim(rows, first, own_buildings, 0)
    counts_own = lax.dynamic_slice_in_dim(counts, first, own_buildings, 0)
    used = (jnp.arange(slot_count, dtype=jnp.int32)[None, :] < counts_own[:, None]).astype(jnp.float32)
    station_prod = rows_own[:, :, None] * waves[None, None, :] % K
    station_angle = station_prod.astype(jnp.float32) * (2.0 * math.pi / K)
    scale = 1.0 / math.sqrt(K)
    t_re = (jnp.cos(station_angle) * scale).astype(jnp.bfloat16).astype(jnp.float32)
    t_im = (-jnp.sin(station_angle) * scale).astype(jnp.bfloat16).astype(jnp.float32)
    w_re = jnp.sum(used[:, :, None] * t_re, axis=1)
    w_im = jnp.sum(used[:, :, None] * t_im, axis=1)

    a_part = w_re * v_re + w_im * v_im
    b_part = w_im * v_re - w_re * v_im
    ab = jnp.concatenate([a_part, b_part], axis=1)
    phase_cat = jnp.concatenate([phase_re, phase_im], axis=0)
    partial = jnp.dot(
        phase_cat.T, ab.T, precision=lax.Precision.HIGHEST, preferred_element_type=jnp.float32
    )
    wave_size = lax.axis_size("wave")
    summed = scatter_sum(partial.reshape(wave_size, case_count // wave_size, own_buildings), "wave", 1)
    return summed.T / counts_own.astype(jnp.float32)[:, None]


def solution(mesh):
    in_specs = (
        P(None, "wave", None, "dof"),
        P(None, "wave", None),
        P(),
        P(),
        P(),
        P(),
        P(None, "dof"),
    )
    out_specs = P("dof", "wave")
    return jax.shard_map(body, mesh=mesh, in_specs=in_specs, out_specs=out_specs, check_vma=False)
```

```python
import math

import jax
import jax.numpy as jnp
from jax import lax
from jax.experimental import pallas as pl
from jax.experimental.pallas import tpu as pltpu
from jax.sharding import PartitionSpec as P

K = 2048


def split_bf16(x):
    hi = x.astype(jnp.bfloat16)
    lo = (x - hi.astype(jnp.float32)).astype(jnp.bfloat16)
    return hi, lo


def scatter_sum(x, axis, collective_id):
    n = x.shape[0]
    block = x.shape[1:]
    mesh_id = pl.DeviceIdType.MESH

    def kernel(x_ref, out_ref, recv, send_sems, recv_sems):
        me = lax.axis_index(axis)
        barrier = pltpu.get_barrier_semaphore()
        for k in range(1, n):
            peer = lax.rem(me + k, n)
            pl.semaphore_signal(barrier, inc=1, device_id={axis: peer}, device_id_type=mesh_id)
        pl.semaphore_wait(barrier, n - 1)
        copies = []
        for k in range(1, n):
            peer = lax.rem(me + k, n)
            copy = pltpu.make_async_remote_copy(
                src_ref=x_ref.at[peer],
                dst_ref=recv.at[k - 1],
                send_sem=send_sems.at[k - 1],
                recv_sem=recv_sems.at[k - 1],
                device_id={axis: peer},
                device_id_type=mesh_id,
            )
            copy.start()
            copies.append(copy)
        for copy in copies:
            copy.wait()
        total = x_ref[me]
        for k in range(n - 1):
            total = total + recv[k]
        out_ref[...] = total

    return pl.pallas_call(
        kernel,
        out_shape=jax.ShapeDtypeStruct(block, x.dtype),
        in_specs=[pl.BlockSpec(memory_space=pltpu.VMEM)],
        out_specs=pl.BlockSpec(memory_space=pltpu.VMEM),
        scratch_shapes=[
            pltpu.VMEM((n - 1,) + block, x.dtype),
            pltpu.SemaphoreType.DMA((n - 1,)),
            pltpu.SemaphoreType.DMA((n - 1,)),
        ],
        compiler_params=pltpu.CompilerParams(collective_id=collective_id, has_side_effects=True),
    )(x)


def dof_exchange(vt, rows_t, used_t, pos_t, load_t, wave_count):
    n = lax.axis_size("dof")
    modes = vt.shape[0]
    own = vt.shape[1] // n
    slots, cases = rows_t.shape[0], pos_t.shape[1]
    axles = pos_t.shape[0]
    mesh_id = pl.DeviceIdType.MESH
    step = 2.0 * math.pi / K
    scale = 1.0 / math.sqrt(K)
    norm_axle = 1.0 / math.sqrt(axles)

    def kernel(vt_ref, rows_ref, used_ref, pos_ref, load_ref, ab_ref, phase_ref, recv, send_sems, recv_sems):
        me = lax.axis_index("dof")
        barrier = pltpu.get_barrier_semaphore()
        for k in range(1, n):
            pl.semaphore_signal(barrier, inc=1, device_id={"dof": lax.rem(me + k, n)}, device_id_type=mesh_id)
        pl.semaphore_wait(barrier, n - 1)
        copies = []
        for k in range(1, n):
            peer = lax.rem(me + k, n)
            copy = pltpu.make_async_remote_copy(
                src_ref=vt_ref.at[:, pl.ds(pl.multiple_of(peer * own, own), own)],
                dst_ref=recv.at[k - 1],
                send_sem=send_sems.at[k - 1],
                recv_sem=recv_sems.at[k - 1],
                device_id={"dof": peer},
                device_id_type=mesh_id,
            )
            copy.start()
            copies.append(copy)

        m_col = lax.axis_index("wave") * wave_count + lax.broadcasted_iota(jnp.int32, (wave_count, 1), 0)
        w_re = jnp.zeros((wave_count, own), jnp.float32)
        w_im = jnp.zeros((wave_count, own), jnp.float32)
        for s in range(slots):
            angle = ((m_col * rows_ref[s : s + 1, :]) & (K - 1)).astype(jnp.float32) * step
            t_re = (jnp.cos(angle) * scale).astype(jnp.bfloat16).astype(jnp.float32)
            t_im = (-jnp.sin(angle) * scale).astype(jnp.bfloat16).astype(jnp.float32)
            used = used_ref[s : s + 1, :]
            w_re = w_re + used * t_re
            w_im = w_im + used * t_im
        p_re = jnp.zeros((wave_count, cases), jnp.float32)
        p_im = jnp.zeros((wave_count, cases), jnp.float32)
        for a in range(axles):
            angle = ((m_col * pos_ref[a : a + 1, :]) & (K - 1)).astype(jnp.float32) * step
            load = load_ref[a : a + 1, :]
            p_re = p_re + load * jnp.cos(angle)
            p_im = p_im + load * jnp.sin(angle)
        phase_ref[0:wave_count, :] = p_re * norm_axle
        phase_ref[wave_count : 2 * wave_count, :] = -p_im * norm_axle

        for copy in copies:
            copy.wait()
        total = vt_ref[:, pl.ds(pl.multiple_of(me * own, own), own)]
        for k in range(n - 1):
            total = total + recv[k]
        v_re = total[0:wave_count]
        v_im = total[wave_count : 2 * wave_count]
        ab_ref[0:wave_count, :] = w_re * v_re + w_im * v_im
        ab_ref[wave_count : 2 * wave_count, :] = w_im * v_re - w_re * v_im

    return pl.pallas_call(
        kernel,
        out_shape=(
            jax.ShapeDtypeStruct((modes, own), jnp.float32),
            jax.ShapeDtypeStruct((2 * wave_count, cases), jnp.float32),
        ),
        in_specs=[pl.BlockSpec(memory_space=pltpu.VMEM)] * 5,
        out_specs=(pl.BlockSpec(memory_space=pltpu.VMEM), pl.BlockSpec(memory_space=pltpu.VMEM)),
        scratch_shapes=[
            pltpu.VMEM((n - 1, modes, own), jnp.float32),
            pltpu.SemaphoreType.DMA((n - 1,)),
            pltpu.SemaphoreType.DMA((n - 1,)),
        ],
        compiler_params=pltpu.CompilerParams(collective_id=0, has_side_effects=True),
    )(vt, rows_t, used_t, pos_t, load_t)


def body(green, rough, axle_pos, axle_load, rows, counts, coupling):
    wave_count = green.shape[1]
    case_count = axle_pos.shape[0]
    building_count = rows.shape[0]
    slot_count = rows.shape[1]
    dof_size = lax.axis_size("dof")
    wave_size = lax.axis_size("wave")
    own_buildings = building_count // dof_size

    re_hi, re_lo = split_bf16(rough[0])
    im_hi, im_lo = split_bf16(rough[1])
    lhs = jnp.stack([re_hi, re_lo, im_hi, im_lo], axis=1)
    prod = jnp.einsum("mkj,gmji->gmki", lhs, green, preferred_element_type=jnp.float32)
    gre_rre = prod[0, :, 0] + prod[0, :, 1]
    gre_rim = prod[0, :, 2] + prod[0, :, 3]
    gim_rre = prod[1, :, 0] + prod[1, :, 1]
    gim_rim = prod[1, :, 2] + prod[1, :, 3]
    h_cat = jnp.concatenate([gre_rre - gim_rim, gre_rim + gim_rre], axis=0)

    h_hi, h_lo = split_bf16(h_cat)
    rhs = jnp.concatenate([h_hi, h_lo], axis=0)
    both = jnp.einsum("ni,bi->nb", rhs, coupling, preferred_element_type=jnp.float32)
    vt_part = both[: 2 * wave_count] + both[2 * wave_count :]

    first = lax.axis_index("dof") * own_buildings
    rows_own = lax.dynamic_slice_in_dim(rows, first, own_buildings, 0)
    counts_own = lax.dynamic_slice_in_dim(counts, first, own_buildings, 0)
    used = (jnp.arange(slot_count, dtype=jnp.int32)[None, :] < counts_own[:, None]).astype(jnp.float32)
    ab_t, phase_cat = dof_exchange(vt_part, rows_own.T, used.T, axle_pos.T, axle_load.T, wave_count)

    partial = lax.dot_general(
        phase_cat, ab_t, (((0,), (0,)), ((), ())),
        precision=lax.Precision.HIGHEST, preferred_element_type=jnp.float32,
    )
    summed = scatter_sum(partial.reshape(wave_size, case_count // wave_size, own_buildings), "wave", 1)
    return summed.T / counts_own.astype(jnp.float32)[:, None]


def solution(mesh):
    in_specs = (
        P(None, "wave", None, "dof"),
        P(None, "wave", None),
        P(),
        P(),
        P(),
        P(),
        P(None, "dof"),
    )
    out_specs = P("dof", "wave")
    return jax.shard_map(body, mesh=mesh, in_specs=in_specs, out_specs=out_specs, check_vma=False)
```

```python
import math

import jax
import jax.numpy as jnp
from jax import lax
from jax.experimental import pallas as pl
from jax.experimental.pallas import tpu as pltpu
from jax.sharding import PartitionSpec as P

K = 2048


def split_bf16(x):
    hi = x.astype(jnp.bfloat16)
    lo = (x - hi.astype(jnp.float32)).astype(jnp.bfloat16)
    return hi, lo


def exchange(vt, rows_t, used_t, pos_t, load_t, wave_count):
    n_dof = lax.axis_size("dof")
    n_wave = lax.axis_size("wave")
    modes = vt.shape[0]
    own = vt.shape[1] // n_dof
    slots, cases = rows_t.shape[0], pos_t.shape[1]
    axles = pos_t.shape[0]
    per_wave = cases // n_wave
    pad = 8
    mesh_id = pl.DeviceIdType.MESH
    step = 2.0 * math.pi / K
    scale = 1.0 / math.sqrt(K)
    norm_axle = 1.0 / math.sqrt(axles)

    def kernel(vt_ref, rows_ref, used_ref, pos_ref, load_ref, out_ref,
               recv_v, send_r, recv_r, v_send, v_recv, r_send, r_recv):
        me_d = lax.axis_index("dof")
        me_w = lax.axis_index("wave")
        barrier = pltpu.get_barrier_semaphore()
        for k in range(1, n_dof):
            pl.semaphore_signal(barrier, inc=1, device_id={"dof": lax.rem(me_d + k, n_dof)}, device_id_type=mesh_id)
        for k in range(1, n_wave):
            pl.semaphore_signal(barrier, inc=1, device_id={"wave": lax.rem(me_w + k, n_wave)}, device_id_type=mesh_id)

        m_col = me_w * wave_count + lax.broadcasted_iota(jnp.int32, (wave_count, 1), 0)
        w_re = jnp.zeros((wave_count, own), jnp.float32)
        w_im = jnp.zeros((wave_count, own), jnp.float32)
        for s in range(slots):
            angle = ((m_col * rows_ref[s : s + 1, :]) & (K - 1)).astype(jnp.float32) * step
            t_re = (jnp.cos(angle) * scale).astype(jnp.bfloat16).astype(jnp.float32)
            t_im = (-jnp.sin(angle) * scale).astype(jnp.bfloat16).astype(jnp.float32)
            used = used_ref[s : s + 1, :]
            w_re = w_re + used * t_re
            w_im = w_im + used * t_im

        pl.semaphore_wait(barrier, n_dof - 1 + n_wave - 1)
        v_copies = []
        for k in range(1, n_dof):
            peer = lax.rem(me_d + k, n_dof)
            copy = pltpu.make_async_remote_copy(
                src_ref=vt_ref.at[:, pl.ds(pl.multiple_of(peer * own, own), own)],
                dst_ref=recv_v.at[k - 1],
                send_sem=v_send.at[k - 1],
                recv_sem=v_recv.at[k - 1],
                device_id={"dof": peer},
                device_id_type=mesh_id,
            )
            copy.start()
            v_copies.append(copy)

        p_re = jnp.zeros((wave_count, cases), jnp.float32)
        p_im = jnp.zeros((wave_count, cases), jnp.float32)
        for a in range(axles):
            angle = ((m_col * pos_ref[a : a + 1, :]) & (K - 1)).astype(jnp.float32) * step
            load = load_ref[a : a + 1, :]
            p_re = p_re + load * jnp.cos(angle)
            p_im = p_im + load * jnp.sin(angle)
        phase = jnp.concatenate([p_re * norm_axle, -p_im * norm_axle], axis=0)

        row = lax.broadcasted_iota(jnp.int32, (n_wave * pad, cases), 0)
        col = lax.broadcasted_iota(jnp.int32, (n_wave * pad, cases), 1)
        spread = jnp.where(
            (col == (row // pad) * per_wave + row % pad) & (row % pad < per_wave), 1.0, 0.0
        ).astype(jnp.bfloat16)
        ph_hi, ph_lo = split_bf16(phase)
        dims = (((1,), (1,)), ((), ()))
        pt_hi = lax.dot_general(spread, ph_hi, dims, preferred_element_type=jnp.float32).astype(jnp.bfloat16)
        pt_lo = lax.dot_general(spread, ph_lo, dims, preferred_element_type=jnp.float32).astype(jnp.bfloat16)

        for copy in v_copies:
            copy.wait()
        total = vt_ref[:, pl.ds(pl.multiple_of(me_d * own, own), own)]
        for k in range(n_dof - 1):
            total = total + recv_v[k]
        v_re = total[0:wave_count]
        v_im = total[wave_count : 2 * wave_count]
        ab = jnp.concatenate([w_re * v_re + w_im * v_im, w_im * v_re - w_re * v_im], axis=0)
        ab_hi, ab_lo = split_bf16(ab)
        r_pad = (
            jnp.dot(pt_hi, ab_hi, preferred_element_type=jnp.float32)
            + jnp.dot(pt_hi, ab_lo, preferred_element_type=jnp.float32)
            + jnp.dot(pt_lo, ab_hi, preferred_element_type=jnp.float32)
        )
        for p in range(n_wave):
            send_r[p] = r_pad[p * pad : (p + 1) * pad]
        result = send_r[me_w]

        r_copies = []
        for k in range(1, n_wave):
            peer = lax.rem(me_w + k, n_wave)
            copy = pltpu.make_async_remote_copy(
                src_ref=send_r.at[peer],
                dst_ref=recv_r.at[k - 1],
                send_sem=r_send.at[k - 1],
                recv_sem=r_recv.at[k - 1],
                device_id={"wave": peer},
                device_id_type=mesh_id,
            )
            copy.start()
            r_copies.append(copy)
        for copy in r_copies:
            copy.wait()
        for k in range(n_wave - 1):
            result = result + recv_r[k]
        out_ref[...] = result

    return pl.pallas_call(
        kernel,
        out_shape=jax.ShapeDtypeStruct((pad, own), jnp.float32),
        in_specs=[pl.BlockSpec(memory_space=pltpu.VMEM)] * 5,
        out_specs=pl.BlockSpec(memory_space=pltpu.VMEM),
        scratch_shapes=[
            pltpu.VMEM((n_dof - 1, modes, own), jnp.float32),
            pltpu.VMEM((n_wave, pad, own), jnp.float32),
            pltpu.VMEM((n_wave - 1, pad, own), jnp.float32),
            pltpu.SemaphoreType.DMA((n_dof - 1,)),
            pltpu.SemaphoreType.DMA((n_dof - 1,)),
            pltpu.SemaphoreType.DMA((n_wave - 1,)),
            pltpu.SemaphoreType.DMA((n_wave - 1,)),
        ],
        compiler_params=pltpu.CompilerParams(collective_id=0, has_side_effects=True),
    )(vt, rows_t, used_t, pos_t, load_t)


def body(green, rough, axle_pos, axle_load, rows, counts, coupling):
    wave_count = green.shape[1]
    case_count = axle_pos.shape[0]
    building_count = rows.shape[0]
    slot_count = rows.shape[1]
    dof_size = lax.axis_size("dof")
    wave_size = lax.axis_size("wave")
    own_buildings = building_count // dof_size

    re_hi, re_lo = split_bf16(rough[0])
    im_hi, im_lo = split_bf16(rough[1])
    lhs = jnp.stack([re_hi, re_lo, im_hi, im_lo], axis=1)
    prod = jnp.einsum("mkj,gmji->gmki", lhs, green, preferred_element_type=jnp.float32)
    gre_rre = prod[0, :, 0] + prod[0, :, 1]
    gre_rim = prod[0, :, 2] + prod[0, :, 3]
    gim_rre = prod[1, :, 0] + prod[1, :, 1]
    gim_rim = prod[1, :, 2] + prod[1, :, 3]
    h_cat = jnp.concatenate([gre_rre - gim_rim, gre_rim + gim_rre], axis=0)

    h_hi, h_lo = split_bf16(h_cat)
    rhs = jnp.concatenate([h_hi, h_lo], axis=0)
    both = jnp.einsum("ni,bi->nb", rhs, coupling, preferred_element_type=jnp.float32)
    vt_part = both[: 2 * wave_count] + both[2 * wave_count :]

    first = lax.axis_index("dof") * own_buildings
    rows_own = lax.dynamic_slice_in_dim(rows, first, own_buildings, 0)
    counts_own = lax.dynamic_slice_in_dim(counts, first, own_buildings, 0)
    used = (jnp.arange(slot_count, dtype=jnp.int32)[None, :] < counts_own[:, None]).astype(jnp.float32)
    summed = exchange(vt_part, rows_own.T, used.T, axle_pos.T, axle_load.T, wave_count)
    per_wave = case_count // wave_size
    return summed[:per_wave].T / counts_own.astype(jnp.float32)[:, None]


def solution(mesh):
    in_specs = (
        P(None, "wave", None, "dof"),
        P(None, "wave", None),
        P(),
        P(),
        P(),
        P(),
        P(None, "dof"),
    )
    out_specs = P("dof", "wave")
    return jax.shard_map(body, mesh=mesh, in_specs=in_specs, out_specs=out_specs, check_vma=False)
```

```python
import math

import jax
import jax.numpy as jnp
from jax import lax
from jax.experimental import pallas as pl
from jax.experimental.pallas import tpu as pltpu
from jax.sharding import PartitionSpec as P

K = 2048


def split_bf16(x):
    hi = x.astype(jnp.bfloat16)
    lo = (x - hi.astype(jnp.float32)).astype(jnp.bfloat16)
    return hi, lo


def exchange(vt, rows_t, pos_t, load_t, wave_count):
    n_dof = lax.axis_size("dof")
    n_wave = lax.axis_size("wave")
    modes = vt.shape[0]
    own = vt.shape[1] // n_dof
    slots, cases = rows_t.shape[0], pos_t.shape[1]
    axles = pos_t.shape[0]
    per_wave = cases // n_wave
    pad = 8
    mesh_id = pl.DeviceIdType.MESH
    step = 2.0 * math.pi / K
    scale = 1.0 / math.sqrt(K)
    norm_axle = 1.0 / math.sqrt(axles)

    def kernel(vt_ref, rows_ref, pos_ref, load_ref, out_ref,
               recv_v, send_r, recv_r, v_send, v_recv, r_send, r_recv):
        me_d = lax.axis_index("dof")
        me_w = lax.axis_index("wave")
        barrier = pltpu.get_barrier_semaphore()
        for k in range(1, n_dof):
            pl.semaphore_signal(barrier, inc=1, device_id={"dof": lax.rem(me_d + k, n_dof)}, device_id_type=mesh_id)
        for k in range(1, n_wave):
            pl.semaphore_signal(barrier, inc=1, device_id={"wave": lax.rem(me_w + k, n_wave)}, device_id_type=mesh_id)

        m_col = me_w * wave_count + lax.broadcasted_iota(jnp.int32, (wave_count, 1), 0)
        w_re = jnp.zeros((wave_count, own), jnp.float32)
        w_im = jnp.zeros((wave_count, own), jnp.float32)
        count = jnp.zeros((1, own), jnp.float32)
        for s in range(slots):
            station = rows_ref[s : s + 1, :]
            angle = ((m_col * station) & (K - 1)).astype(jnp.float32) * step
            t_re = (jnp.cos(angle) * scale).astype(jnp.bfloat16).astype(jnp.float32)
            t_im = (-jnp.sin(angle) * scale).astype(jnp.bfloat16).astype(jnp.float32)
            used = jnp.where(station >= 0, 1.0, 0.0)
            count = count + used
            w_re = w_re + used * t_re
            w_im = w_im + used * t_im

        pl.semaphore_wait(barrier, n_dof - 1 + n_wave - 1)
        v_copies = []
        for k in range(1, n_dof):
            peer = lax.rem(me_d + k, n_dof)
            copy = pltpu.make_async_remote_copy(
                src_ref=vt_ref.at[:, pl.ds(pl.multiple_of(peer * own, own), own)],
                dst_ref=recv_v.at[k - 1],
                send_sem=v_send.at[k - 1],
                recv_sem=v_recv.at[k - 1],
                device_id={"dof": peer},
                device_id_type=mesh_id,
            )
            copy.start()
            v_copies.append(copy)

        p_re = jnp.zeros((wave_count, cases), jnp.float32)
        p_im = jnp.zeros((wave_count, cases), jnp.float32)
        for a in range(axles):
            angle = ((m_col * pos_ref[a : a + 1, :]) & (K - 1)).astype(jnp.float32) * step
            load = load_ref[a : a + 1, :]
            p_re = p_re + load * jnp.cos(angle)
            p_im = p_im + load * jnp.sin(angle)
        phase = jnp.concatenate([p_re * norm_axle, -p_im * norm_axle], axis=0)

        row = lax.broadcasted_iota(jnp.int32, (n_wave * pad, cases), 0)
        col = lax.broadcasted_iota(jnp.int32, (n_wave * pad, cases), 1)
        spread = jnp.where(
            (col == (row // pad) * per_wave + row % pad) & (row % pad < per_wave), 1.0, 0.0
        ).astype(jnp.bfloat16)
        ph_hi, ph_lo = split_bf16(phase)
        dims = (((1,), (1,)), ((), ()))
        pt_hi = lax.dot_general(spread, ph_hi, dims, preferred_element_type=jnp.float32).astype(jnp.bfloat16)
        pt_lo = lax.dot_general(spread, ph_lo, dims, preferred_element_type=jnp.float32).astype(jnp.bfloat16)

        for copy in v_copies:
            copy.wait()
        total = vt_ref[:, pl.ds(pl.multiple_of(me_d * own, own), own)]
        for k in range(n_dof - 1):
            total = total + recv_v[k]
        v_re = total[0:wave_count]
        v_im = total[wave_count : 2 * wave_count]
        ab = jnp.concatenate([w_re * v_re + w_im * v_im, w_im * v_re - w_re * v_im], axis=0)
        ab_hi, ab_lo = split_bf16(ab)
        r_pad = (
            jnp.dot(pt_hi, ab_hi, preferred_element_type=jnp.float32)
            + jnp.dot(pt_hi, ab_lo, preferred_element_type=jnp.float32)
            + jnp.dot(pt_lo, ab_hi, preferred_element_type=jnp.float32)
        )
        for p in range(n_wave):
            send_r[p] = r_pad[p * pad : (p + 1) * pad]
        result = send_r[me_w]

        r_copies = []
        for k in range(1, n_wave):
            peer = lax.rem(me_w + k, n_wave)
            copy = pltpu.make_async_remote_copy(
                src_ref=send_r.at[peer, 0:per_wave],
                dst_ref=recv_r.at[k - 1, 0:per_wave],
                send_sem=r_send.at[k - 1],
                recv_sem=r_recv.at[k - 1],
                device_id={"wave": peer},
                device_id_type=mesh_id,
            )
            copy.start()
            r_copies.append(copy)
        for copy in r_copies:
            copy.wait()
        result = result[0:per_wave]
        for k in range(n_wave - 1):
            result = result + recv_r[k, 0:per_wave]
        out_ref[...] = result / count

    return pl.pallas_call(
        kernel,
        out_shape=jax.ShapeDtypeStruct((per_wave, own), jnp.float32),
        in_specs=[pl.BlockSpec(memory_space=pltpu.VMEM)] * 4,
        out_specs=pl.BlockSpec(memory_space=pltpu.VMEM),
        scratch_shapes=[
            pltpu.VMEM((n_dof - 1, modes, own), jnp.float32),
            pltpu.VMEM((n_wave, pad, own), jnp.float32),
            pltpu.VMEM((n_wave - 1, pad, own), jnp.float32),
            pltpu.SemaphoreType.DMA((n_dof - 1,)),
            pltpu.SemaphoreType.DMA((n_dof - 1,)),
            pltpu.SemaphoreType.DMA((n_wave - 1,)),
            pltpu.SemaphoreType.DMA((n_wave - 1,)),
        ],
        compiler_params=pltpu.CompilerParams(collective_id=0, has_side_effects=True),
    )(vt, rows_t, pos_t, load_t)


def body(green, rough, axle_pos, axle_load, rows, counts, coupling):
    wave_count = green.shape[1]
    case_count = axle_pos.shape[0]
    building_count = rows.shape[0]
    slot_count = rows.shape[1]
    dof_size = lax.axis_size("dof")
    wave_size = lax.axis_size("wave")
    own_buildings = building_count // dof_size

    re_hi, re_lo = split_bf16(rough[0])
    im_hi, im_lo = split_bf16(rough[1])
    lhs = jnp.stack([re_hi, re_lo, im_hi, im_lo], axis=1)
    prod = jnp.einsum("mkj,gmji->gmki", lhs, green, preferred_element_type=jnp.float32)
    gre_rre = prod[0, :, 0] + prod[0, :, 1]
    gre_rim = prod[0, :, 2] + prod[0, :, 3]
    gim_rre = prod[1, :, 0] + prod[1, :, 1]
    gim_rim = prod[1, :, 2] + prod[1, :, 3]
    h_cat = jnp.concatenate([gre_rre - gim_rim, gre_rim + gim_rre], axis=0)

    h_hi, h_lo = split_bf16(h_cat)
    rhs = jnp.concatenate([h_hi, h_lo], axis=0)
    both = jnp.einsum("ni,bi->nb", rhs, coupling, preferred_element_type=jnp.float32)
    vt_part = both[: 2 * wave_count] + both[2 * wave_count :]

    first = lax.axis_index("dof") * own_buildings
    rows_own = lax.dynamic_slice_in_dim(rows, first, own_buildings, 0)
    counts_own = lax.dynamic_slice_in_dim(counts, first, own_buildings, 0)
    rows_used = jnp.where(
        jnp.arange(slot_count, dtype=jnp.int32)[:, None] < counts_own[None, :], rows_own.T, -1
    )
    return exchange(vt_part, rows_used, axle_pos.T, axle_load.T, wave_count).T


def solution(mesh):
    in_specs = (
        P(None, "wave", None, "dof"),
        P(None, "wave", None),
        P(),
        P(),
        P(),
        P(),
        P(None, "dof"),
    )
    out_specs = P("dof", "wave")
    return jax.shard_map(body, mesh=mesh, in_specs=in_specs, out_specs=out_specs, check_vma=False)
```

```python
import math

import jax
import jax.numpy as jnp
from jax import lax
from jax.experimental import pallas as pl
from jax.experimental.pallas import tpu as pltpu
from jax.sharding import PartitionSpec as P

K = 2048


def split_bf16(x):
    hi = x.astype(jnp.bfloat16)
    lo = (x - hi.astype(jnp.float32)).astype(jnp.bfloat16)
    return hi, lo


def exchange(vt, rows_t, pos_t, load_t, wave_count):
    n_dof = lax.axis_size("dof")
    n_wave = lax.axis_size("wave")
    modes = vt.shape[0]
    own = vt.shape[1] // n_dof
    slots, cases = rows_t.shape[0], pos_t.shape[1]
    axles = pos_t.shape[0]
    per_wave = cases // n_wave
    pad = 8
    mesh_id = pl.DeviceIdType.MESH
    step = 2.0 * math.pi / K
    scale = 1.0 / math.sqrt(K)
    norm_axle = 1.0 / math.sqrt(axles)
    group = 8
    groups = wave_count // group

    def turns(m_first, station):
        v_col = lax.broadcasted_iota(jnp.int32, (group, 1), 0)
        coarse = (((m_first + group * v_col) * station) & (K - 1)).astype(jnp.float32) * step
        fine = ((v_col * station) & (K - 1)).astype(jnp.float32) * step
        c_coarse, s_coarse = jnp.cos(coarse), jnp.sin(coarse)
        c_fine, s_fine = jnp.cos(fine), jnp.sin(fine)
        blocks = []
        for u in range(groups):
            cu = c_coarse[u : u + 1, :]
            su = s_coarse[u : u + 1, :]
            blocks.append((cu * c_fine - su * s_fine, su * c_fine + cu * s_fine))
        return blocks

    def kernel(vt_ref, rows_ref, pos_ref, load_ref, out_ref,
               recv_v, send_r, recv_r, v_send, v_recv, r_send, r_recv):
        me_d = lax.axis_index("dof")
        me_w = lax.axis_index("wave")
        barrier = pltpu.get_barrier_semaphore()
        for k in range(1, n_dof):
            pl.semaphore_signal(barrier, inc=1, device_id={"dof": lax.rem(me_d + k, n_dof)}, device_id_type=mesh_id)
        for k in range(1, n_wave):
            pl.semaphore_signal(barrier, inc=1, device_id={"wave": lax.rem(me_w + k, n_wave)}, device_id_type=mesh_id)

        m_first = me_w * wave_count
        count = jnp.zeros((1, own), jnp.float32)
        w_re = [jnp.zeros((group, own), jnp.float32) for _ in range(groups)]
        w_im = [jnp.zeros((group, own), jnp.float32) for _ in range(groups)]
        for s in range(slots):
            station = rows_ref[s : s + 1, :]
            used = jnp.where(station >= 0, 1.0, 0.0)
            count = count + used
            for u, (c, sn) in enumerate(turns(m_first, station)):
                t_re = (c * scale).astype(jnp.bfloat16).astype(jnp.float32)
                t_im = (-sn * scale).astype(jnp.bfloat16).astype(jnp.float32)
                w_re[u] = w_re[u] + used * t_re
                w_im[u] = w_im[u] + used * t_im
        w_re = jnp.concatenate(w_re, axis=0)
        w_im = jnp.concatenate(w_im, axis=0)

        pl.semaphore_wait(barrier, n_dof - 1 + n_wave - 1)
        v_copies = []
        for k in range(1, n_dof):
            peer = lax.rem(me_d + k, n_dof)
            copy = pltpu.make_async_remote_copy(
                src_ref=vt_ref.at[:, pl.ds(pl.multiple_of(peer * own, own), own)],
                dst_ref=recv_v.at[k - 1],
                send_sem=v_send.at[k - 1],
                recv_sem=v_recv.at[k - 1],
                device_id={"dof": peer},
                device_id_type=mesh_id,
            )
            copy.start()
            v_copies.append(copy)

        p_re = [jnp.zeros((group, cases), jnp.float32) for _ in range(groups)]
        p_im = [jnp.zeros((group, cases), jnp.float32) for _ in range(groups)]
        for a in range(axles):
            load = load_ref[a : a + 1, :]
            for u, (c, sn) in enumerate(turns(m_first, pos_ref[a : a + 1, :])):
                p_re[u] = p_re[u] + load * c
                p_im[u] = p_im[u] + load * sn
        p_re = jnp.concatenate(p_re, axis=0)
        p_im = jnp.concatenate(p_im, axis=0)
        phase = jnp.concatenate([p_re * norm_axle, -p_im * norm_axle], axis=0)

        row = lax.broadcasted_iota(jnp.int32, (n_wave * pad, cases), 0)
        col = lax.broadcasted_iota(jnp.int32, (n_wave * pad, cases), 1)
        spread = jnp.where(
            (col == (row // pad) * per_wave + row % pad) & (row % pad < per_wave), 1.0, 0.0
        ).astype(jnp.bfloat16)
        ph_hi, ph_lo = split_bf16(phase)
        dims = (((1,), (1,)), ((), ()))
        pt_hi = lax.dot_general(spread, ph_hi, dims, preferred_element_type=jnp.float32).astype(jnp.bfloat16)
        pt_lo = lax.dot_general(spread, ph_lo, dims, preferred_element_type=jnp.float32).astype(jnp.bfloat16)

        for copy in v_copies:
            copy.wait()
        total = vt_ref[:, pl.ds(pl.multiple_of(me_d * own, own), own)]
        for k in range(n_dof - 1):
            total = total + recv_v[k]
        v_re = total[0:wave_count]
        v_im = total[wave_count : 2 * wave_count]
        ab = jnp.concatenate([w_re * v_re + w_im * v_im, w_im * v_re - w_re * v_im], axis=0)
        ab_hi, ab_lo = split_bf16(ab)
        r_pad = (
            jnp.dot(pt_hi, ab_hi, preferred_element_type=jnp.float32)
            + jnp.dot(pt_hi, ab_lo, preferred_element_type=jnp.float32)
            + jnp.dot(pt_lo, ab_hi, preferred_element_type=jnp.float32)
        )
        for p in range(n_wave):
            send_r[p] = r_pad[p * pad : (p + 1) * pad]
        result = send_r[me_w]

        r_copies = []
        for k in range(1, n_wave):
            peer = lax.rem(me_w + k, n_wave)
            copy = pltpu.make_async_remote_copy(
                src_ref=send_r.at[peer, 0:per_wave],
                dst_ref=recv_r.at[k - 1, 0:per_wave],
                send_sem=r_send.at[k - 1],
                recv_sem=r_recv.at[k - 1],
                device_id={"wave": peer},
                device_id_type=mesh_id,
            )
            copy.start()
            r_copies.append(copy)
        for copy in r_copies:
            copy.wait()
        result = result[0:per_wave]
        for k in range(n_wave - 1):
            result = result + recv_r[k, 0:per_wave]
        out_ref[...] = result / count

    return pl.pallas_call(
        kernel,
        out_shape=jax.ShapeDtypeStruct((per_wave, own), jnp.float32),
        in_specs=[pl.BlockSpec(memory_space=pltpu.VMEM)] * 4,
        out_specs=pl.BlockSpec(memory_space=pltpu.VMEM),
        scratch_shapes=[
            pltpu.VMEM((n_dof - 1, modes, own), jnp.float32),
            pltpu.VMEM((n_wave, pad, own), jnp.float32),
            pltpu.VMEM((n_wave - 1, pad, own), jnp.float32),
            pltpu.SemaphoreType.DMA((n_dof - 1,)),
            pltpu.SemaphoreType.DMA((n_dof - 1,)),
            pltpu.SemaphoreType.DMA((n_wave - 1,)),
            pltpu.SemaphoreType.DMA((n_wave - 1,)),
        ],
        compiler_params=pltpu.CompilerParams(collective_id=0, has_side_effects=True),
    )(vt, rows_t, pos_t, load_t)


def body(green, rough, axle_pos, axle_load, rows, counts, coupling):
    wave_count = green.shape[1]
    case_count = axle_pos.shape[0]
    building_count = rows.shape[0]
    slot_count = rows.shape[1]
    dof_size = lax.axis_size("dof")
    wave_size = lax.axis_size("wave")
    own_buildings = building_count // dof_size

    re_hi, re_lo = split_bf16(rough[0])
    im_hi, im_lo = split_bf16(rough[1])
    lhs = jnp.stack([re_hi, re_lo, im_hi, im_lo], axis=1)
    prod = jnp.einsum("mkj,gmji->gmki", lhs, green, preferred_element_type=jnp.float32)
    gre_rre = prod[0, :, 0] + prod[0, :, 1]
    gre_rim = prod[0, :, 2] + prod[0, :, 3]
    gim_rre = prod[1, :, 0] + prod[1, :, 1]
    gim_rim = prod[1, :, 2] + prod[1, :, 3]
    h_cat = jnp.concatenate([gre_rre - gim_rim, gre_rim + gim_rre], axis=0)

    h_hi, h_lo = split_bf16(h_cat)
    rhs = jnp.concatenate([h_hi, h_lo], axis=0)
    both = jnp.einsum("ni,bi->nb", rhs, coupling, preferred_element_type=jnp.float32)
    vt_part = both[: 2 * wave_count] + both[2 * wave_count :]

    first = lax.axis_index("dof") * own_buildings
    rows_own = lax.dynamic_slice_in_dim(rows, first, own_buildings, 0)
    counts_own = lax.dynamic_slice_in_dim(counts, first, own_buildings, 0)
    rows_used = jnp.where(
        jnp.arange(slot_count, dtype=jnp.int32)[:, None] < counts_own[None, :], rows_own.T, -1
    )
    return exchange(vt_part, rows_used, axle_pos.T, axle_load.T, wave_count).T


def solution(mesh):
    in_specs = (
        P(None, "wave", None, "dof"),
        P(None, "wave", None),
        P(),
        P(),
        P(),
        P(),
        P(None, "dof"),
    )
    out_specs = P("dof", "wave")
    return jax.shard_map(body, mesh=mesh, in_specs=in_specs, out_specs=out_specs, check_vma=False)
```

```python
import math

import jax
import jax.numpy as jnp
from jax import lax
from jax.experimental import pallas as pl
from jax.experimental.pallas import tpu as pltpu
from jax.sharding import PartitionSpec as P

K = 2048


def split_bf16(x):
    hi = x.astype(jnp.bfloat16)
    lo = (x - hi.astype(jnp.float32)).astype(jnp.bfloat16)
    return hi, lo


def exchange(vt, rows_t, counts_row, pos_t, load_t, wave_count):
    n_dof = lax.axis_size("dof")
    n_wave = lax.axis_size("wave")
    modes = vt.shape[0]
    own = vt.shape[1] // n_dof
    slots, cases = rows_t.shape[0], pos_t.shape[1]
    axles = pos_t.shape[0]
    per_wave = cases // n_wave
    pad = 8
    mesh_id = pl.DeviceIdType.MESH
    step = 2.0 * math.pi / K
    scale = 1.0 / math.sqrt(K)
    norm_axle = 1.0 / math.sqrt(axles)
    group = 8
    groups = wave_count // group

    def turns(m_first, station):
        v_col = lax.broadcasted_iota(jnp.int32, (group, 1), 0)
        coarse = (((m_first + group * v_col) * station) & (K - 1)).astype(jnp.float32) * step
        fine = ((v_col * station) & (K - 1)).astype(jnp.float32) * step
        c_coarse, s_coarse = jnp.cos(coarse), jnp.sin(coarse)
        c_fine, s_fine = jnp.cos(fine), jnp.sin(fine)
        blocks = []
        for u in range(groups):
            cu = c_coarse[u : u + 1, :]
            su = s_coarse[u : u + 1, :]
            blocks.append((cu * c_fine - su * s_fine, su * c_fine + cu * s_fine))
        return blocks

    def kernel(vt_ref, rows_ref, counts_ref, pos_ref, load_ref, out_ref,
               recv_v, send_r, recv_r, v_send, v_recv, r_send, r_recv):
        me_d = lax.axis_index("dof")
        me_w = lax.axis_index("wave")
        barrier = pltpu.get_barrier_semaphore()
        for k in range(1, n_dof):
            pl.semaphore_signal(barrier, inc=1, device_id={"dof": lax.rem(me_d + k, n_dof)}, device_id_type=mesh_id)
        for k in range(1, n_wave):
            pl.semaphore_signal(barrier, inc=1, device_id={"wave": lax.rem(me_w + k, n_wave)}, device_id_type=mesh_id)

        pl.semaphore_wait(barrier, n_dof - 1 + n_wave - 1)
        v_copies = []
        for k in range(1, n_dof):
            peer = lax.rem(me_d + k, n_dof)
            copy = pltpu.make_async_remote_copy(
                src_ref=vt_ref.at[:, pl.ds(pl.multiple_of(peer * own, own), own)],
                dst_ref=recv_v.at[k - 1],
                send_sem=v_send.at[k - 1],
                recv_sem=v_recv.at[k - 1],
                device_id={"dof": peer},
                device_id_type=mesh_id,
            )
            copy.start()
            v_copies.append(copy)

        m_first = me_w * wave_count
        mine = pl.ds(pl.multiple_of(me_d * own, own), own)
        count = counts_ref[:, mine]
        w_re = [jnp.zeros((group, own), jnp.float32) for _ in range(groups)]
        w_im = [jnp.zeros((group, own), jnp.float32) for _ in range(groups)]
        for s in range(slots):
            station = rows_ref[s : s + 1, mine]
            used = jnp.where(count > s, 1.0, 0.0)
            for u, (c, sn) in enumerate(turns(m_first, station)):
                t_re = (c * scale).astype(jnp.bfloat16).astype(jnp.float32)
                t_im = (-sn * scale).astype(jnp.bfloat16).astype(jnp.float32)
                w_re[u] = w_re[u] + used * t_re
                w_im[u] = w_im[u] + used * t_im
        w_re = jnp.concatenate(w_re, axis=0)
        w_im = jnp.concatenate(w_im, axis=0)

        p_re = [jnp.zeros((group, cases), jnp.float32) for _ in range(groups)]
        p_im = [jnp.zeros((group, cases), jnp.float32) for _ in range(groups)]
        for a in range(axles):
            load = load_ref[a : a + 1, :]
            for u, (c, sn) in enumerate(turns(m_first, pos_ref[a : a + 1, :])):
                p_re[u] = p_re[u] + load * c
                p_im[u] = p_im[u] + load * sn
        p_re = jnp.concatenate(p_re, axis=0)
        p_im = jnp.concatenate(p_im, axis=0)
        phase = jnp.concatenate([p_re * norm_axle, -p_im * norm_axle], axis=0)

        row = lax.broadcasted_iota(jnp.int32, (n_wave * pad, cases), 0)
        col = lax.broadcasted_iota(jnp.int32, (n_wave * pad, cases), 1)
        spread = jnp.where(
            (col == (row // pad) * per_wave + row % pad) & (row % pad < per_wave), 1.0, 0.0
        ).astype(jnp.bfloat16)
        ph_hi, ph_lo = split_bf16(phase)
        dims = (((1,), (1,)), ((), ()))
        pt_hi = lax.dot_general(spread, ph_hi, dims, preferred_element_type=jnp.float32).astype(jnp.bfloat16)
        pt_lo = lax.dot_general(spread, ph_lo, dims, preferred_element_type=jnp.float32).astype(jnp.bfloat16)

        for copy in v_copies:
            copy.wait()
        total = vt_ref[:, pl.ds(pl.multiple_of(me_d * own, own), own)]
        for k in range(n_dof - 1):
            total = total + recv_v[k]
        v_re = total[0:wave_count]
        v_im = total[wave_count : 2 * wave_count]
        ab = jnp.concatenate([w_re * v_re + w_im * v_im, w_im * v_re - w_re * v_im], axis=0)
        ab_hi, ab_lo = split_bf16(ab)
        r_pad = (
            jnp.dot(pt_hi, ab_hi, preferred_element_type=jnp.float32)
            + jnp.dot(pt_hi, ab_lo, preferred_element_type=jnp.float32)
            + jnp.dot(pt_lo, ab_hi, preferred_element_type=jnp.float32)
        )
        for p in range(n_wave):
            send_r[p] = r_pad[p * pad : (p + 1) * pad]
        result = send_r[me_w]

        r_copies = []
        for k in range(1, n_wave):
            peer = lax.rem(me_w + k, n_wave)
            copy = pltpu.make_async_remote_copy(
                src_ref=send_r.at[peer, 0:per_wave],
                dst_ref=recv_r.at[k - 1, 0:per_wave],
                send_sem=r_send.at[k - 1],
                recv_sem=r_recv.at[k - 1],
                device_id={"wave": peer},
                device_id_type=mesh_id,
            )
            copy.start()
            r_copies.append(copy)
        for copy in r_copies:
            copy.wait()
        result = result[0:per_wave]
        for k in range(n_wave - 1):
            result = result + recv_r[k, 0:per_wave]
        out_ref[...] = result / count.astype(jnp.float32)

    return pl.pallas_call(
        kernel,
        out_shape=jax.ShapeDtypeStruct((per_wave, own), jnp.float32),
        in_specs=[pl.BlockSpec(memory_space=pltpu.VMEM)] * 5,
        out_specs=pl.BlockSpec(memory_space=pltpu.VMEM),
        scratch_shapes=[
            pltpu.VMEM((n_dof - 1, modes, own), jnp.float32),
            pltpu.VMEM((n_wave, pad, own), jnp.float32),
            pltpu.VMEM((n_wave - 1, pad, own), jnp.float32),
            pltpu.SemaphoreType.DMA((n_dof - 1,)),
            pltpu.SemaphoreType.DMA((n_dof - 1,)),
            pltpu.SemaphoreType.DMA((n_wave - 1,)),
            pltpu.SemaphoreType.DMA((n_wave - 1,)),
        ],
        compiler_params=pltpu.CompilerParams(collective_id=0, has_side_effects=True),
    )(vt, rows_t, counts_row, pos_t, load_t)


def body(green, rough, axle_pos, axle_load, rows, counts, coupling):
    wave_count = green.shape[1]
    case_count = axle_pos.shape[0]
    building_count = rows.shape[0]
    slot_count = rows.shape[1]
    dof_size = lax.axis_size("dof")
    wave_size = lax.axis_size("wave")
    own_buildings = building_count // dof_size

    re_hi, re_lo = split_bf16(rough[0])
    im_hi, im_lo = split_bf16(rough[1])
    lhs = jnp.stack([re_hi, re_lo, im_hi, im_lo], axis=1)
    prod = jnp.einsum("mkj,gmji->gmki", lhs, green, preferred_element_type=jnp.float32)
    gre_rre = prod[0, :, 0] + prod[0, :, 1]
    gre_rim = prod[0, :, 2] + prod[0, :, 3]
    gim_rre = prod[1, :, 0] + prod[1, :, 1]
    gim_rim = prod[1, :, 2] + prod[1, :, 3]
    h_cat = jnp.concatenate([gre_rre - gim_rim, gre_rim + gim_rre], axis=0)

    vt_part = lax.dot_general(
        h_cat, coupling, (((1,), (1,)), ((), ())),
        precision=lax.Precision.HIGHEST, preferred_element_type=jnp.float32,
    )
    return exchange(vt_part, rows.T, counts.reshape(1, -1), axle_pos.T, axle_load.T, wave_count).T


def solution(mesh):
    in_specs = (
        P(None, "wave", None, "dof"),
        P(None, "wave", None),
        P(),
        P(),
        P(),
        P(),
        P(None, "dof"),
    )
    out_specs = P("dof", "wave")
    return jax.shard_map(body, mesh=mesh, in_specs=in_specs, out_specs=out_specs, check_vma=False)
```

```python
import math

import jax
import jax.numpy as jnp
from jax import lax
from jax.experimental import pallas as pl
from jax.experimental.pallas import tpu as pltpu
from jax.sharding import PartitionSpec as P

K = 2048


def split_bf16(x):
    hi = x.astype(jnp.bfloat16)
    lo = (x - hi.astype(jnp.float32)).astype(jnp.bfloat16)
    return hi, lo


def exchange(green, lhs, coupling, rows_t, counts_row, pos_t, load_t):
    n_dof = lax.axis_size("dof")
    n_wave = lax.axis_size("wave")
    wave_count = green.shape[1]
    modes = 2 * wave_count
    dofs = green.shape[3]
    forcing = green.shape[2]
    own = coupling.shape[0] // n_dof
    block = 8
    blocks = wave_count // block
    slots, cases = rows_t.shape[0], pos_t.shape[1]
    axles = pos_t.shape[0]
    per_wave = cases // n_wave
    pad = 8
    mesh_id = pl.DeviceIdType.MESH
    step = 2.0 * math.pi / K
    scale = 1.0 / math.sqrt(K)
    norm_axle = 1.0 / math.sqrt(axles)
    group = 8
    groups = wave_count // group

    def turns(m_first, station):
        v_col = lax.broadcasted_iota(jnp.int32, (group, 1), 0)
        coarse = (((m_first + group * v_col) * station) & (K - 1)).astype(jnp.float32) * step
        fine = ((v_col * station) & (K - 1)).astype(jnp.float32) * step
        c_coarse, s_coarse = jnp.cos(coarse), jnp.sin(coarse)
        c_fine, s_fine = jnp.cos(fine), jnp.sin(fine)
        blocks = []
        for u in range(groups):
            cu = c_coarse[u : u + 1, :]
            su = s_coarse[u : u + 1, :]
            blocks.append((cu * c_fine - su * s_fine, su * c_fine + cu * s_fine))
        return blocks

    def kernel(green_hbm, lhs_ref, cpl_ref, rows_ref, counts_ref, pos_ref, load_ref, out_ref,
               gbuf, gsem, raw, h_send, recv_h, recv_c, send_r, recv_r,
               h_sems, c_sems, r_send, r_recv):
        me_d = lax.axis_index("dof")
        me_w = lax.axis_index("wave")
        barrier = pltpu.get_barrier_semaphore()
        for k in range(1, n_dof):
            pl.semaphore_signal(barrier, inc=1, device_id={"dof": lax.rem(me_d + k, n_dof)}, device_id_type=mesh_id)
        for k in range(1, n_wave):
            pl.semaphore_signal(barrier, inc=1, device_id={"wave": lax.rem(me_w + k, n_wave)}, device_id_type=mesh_id)

        def fetch(t, slot):
            pltpu.make_async_copy(
                green_hbm.at[:, pl.ds(pl.multiple_of(t * block, block), block)], gbuf.at[slot], gsem.at[slot]
            ).start()

        fetch(0, 0)
        pl.semaphore_wait(barrier, n_dof - 1 + n_wave - 1)

        def remote(src_ref, dst_ref, sems, k, peer):
            return pltpu.make_async_remote_copy(
                src_ref=src_ref, dst_ref=dst_ref, send_sem=sems.at[0, k - 1], recv_sem=sems.at[1, k - 1],
                device_id={"dof": peer}, device_id_type=mesh_id,
            )

        c_copies = []
        for k in range(1, n_dof):
            peer = lax.rem(me_d + k, n_dof)
            copy = remote(cpl_ref.at[pl.ds(pl.multiple_of(peer * own, own), own)], recv_c.at[k - 1], c_sems, k, peer)
            copy.start()
            c_copies.append(copy)

        def matvec(t, carry):
            slot = lax.rem(t, 2)
            pltpu.make_async_copy(green_hbm.at[:, pl.ds(0, block)], gbuf.at[slot], gsem.at[slot]).wait()

            @pl.when(t + 1 < blocks)
            def _():
                fetch(t + 1, 1 - slot)

            first = pl.multiple_of(t * block, block)
            for mm in range(block):
                l = lhs_ref[first + mm]
                for g in range(2):
                    raw[g, first + mm] = jnp.dot(l, gbuf[slot, g, mm], preferred_element_type=jnp.float32)
            return carry

        lax.fori_loop(0, blocks, matvec, 0)
        gre_rre = raw[0, :, 0, :] + raw[0, :, 1, :]
        gre_rim = raw[0, :, 2, :] + raw[0, :, 3, :]
        gim_rre = raw[1, :, 0, :] + raw[1, :, 1, :]
        gim_rim = raw[1, :, 2, :] + raw[1, :, 3, :]
        h_send[0:wave_count, :] = gre_rre - gim_rim
        h_send[wave_count:modes, :] = gre_rim + gim_rre
        h_copies = []
        for k in range(1, n_dof):
            peer = lax.rem(me_d + k, n_dof)
            copy = remote(h_send, recv_h.at[k - 1], h_sems, k, peer)
            copy.start()
            h_copies.append(copy)

        m_first = me_w * wave_count
        mine = pl.ds(pl.multiple_of(me_d * own, own), own)
        count = counts_ref[:, mine]
        w_re = [jnp.zeros((group, own), jnp.float32) for _ in range(groups)]
        w_im = [jnp.zeros((group, own), jnp.float32) for _ in range(groups)]
        for s in range(slots):
            station = rows_ref[s : s + 1, mine]
            used = jnp.where(count > s, 1.0, 0.0)
            for u, (c, sn) in enumerate(turns(m_first, station)):
                t_re = (c * scale).astype(jnp.bfloat16).astype(jnp.float32)
                t_im = (-sn * scale).astype(jnp.bfloat16).astype(jnp.float32)
                w_re[u] = w_re[u] + used * t_re
                w_im[u] = w_im[u] + used * t_im
        w_re = jnp.concatenate(w_re, axis=0)
        w_im = jnp.concatenate(w_im, axis=0)

        p_re = [jnp.zeros((group, cases), jnp.float32) for _ in range(groups)]
        p_im = [jnp.zeros((group, cases), jnp.float32) for _ in range(groups)]
        for a in range(axles):
            load = load_ref[a : a + 1, :]
            for u, (c, sn) in enumerate(turns(m_first, pos_ref[a : a + 1, :])):
                p_re[u] = p_re[u] + load * c
                p_im[u] = p_im[u] + load * sn
        p_re = jnp.concatenate(p_re, axis=0)
        p_im = jnp.concatenate(p_im, axis=0)
        phase = jnp.concatenate([p_re * norm_axle, -p_im * norm_axle], axis=0)

        row = lax.broadcasted_iota(jnp.int32, (n_wave * pad, cases), 0)
        col = lax.broadcasted_iota(jnp.int32, (n_wave * pad, cases), 1)
        spread = jnp.where(
            (col == (row // pad) * per_wave + row % pad) & (row % pad < per_wave), 1.0, 0.0
        ).astype(jnp.bfloat16)
        ph_hi, ph_lo = split_bf16(phase)
        dims = (((1,), (1,)), ((), ()))
        pt_hi = lax.dot_general(spread, ph_hi, dims, preferred_element_type=jnp.float32).astype(jnp.bfloat16)
        pt_lo = lax.dot_general(spread, ph_lo, dims, preferred_element_type=jnp.float32).astype(jnp.bfloat16)

        mine_rows = pl.ds(pl.multiple_of(me_d * own, own), own)
        dims_t = (((1,), (1,)), ((), ()))

        def v_term(h, c):
            h_hi, h_lo = split_bf16(h)
            return (lax.dot_general(h_hi, c, dims_t, preferred_element_type=jnp.float32)
                    + lax.dot_general(h_lo, c, dims_t, preferred_element_type=jnp.float32))

        total = v_term(h_send[...], cpl_ref[mine_rows, :])
        for copy in c_copies + h_copies:
            copy.wait()
        for k in range(n_dof - 1):
            total = total + v_term(recv_h[k], recv_c[k])
        v_re = total[0:wave_count]
        v_im = total[wave_count : 2 * wave_count]
        ab = jnp.concatenate([w_re * v_re + w_im * v_im, w_im * v_re - w_re * v_im], axis=0)
        ab_hi, ab_lo = split_bf16(ab)
        r_pad = (
            jnp.dot(pt_hi, ab_hi, preferred_element_type=jnp.float32)
            + jnp.dot(pt_hi, ab_lo, preferred_element_type=jnp.float32)
            + jnp.dot(pt_lo, ab_hi, preferred_element_type=jnp.float32)
        )
        for p in range(n_wave):
            send_r[p] = r_pad[p * pad : (p + 1) * pad]
        result = send_r[me_w]

        r_copies = []
        for k in range(1, n_wave):
            peer = lax.rem(me_w + k, n_wave)
            copy = pltpu.make_async_remote_copy(
                src_ref=send_r.at[peer, 0:per_wave],
                dst_ref=recv_r.at[k - 1, 0:per_wave],
                send_sem=r_send.at[k - 1],
                recv_sem=r_recv.at[k - 1],
                device_id={"wave": peer},
                device_id_type=mesh_id,
            )
            copy.start()
            r_copies.append(copy)
        for copy in r_copies:
            copy.wait()
        result = result[0:per_wave]
        for k in range(n_wave - 1):
            result = result + recv_r[k, 0:per_wave]
        out_ref[...] = result / count.astype(jnp.float32)

    return pl.pallas_call(
        kernel,
        out_shape=jax.ShapeDtypeStruct((per_wave, own), jnp.float32),
        in_specs=[pl.BlockSpec(memory_space=pl.ANY)] + [pl.BlockSpec(memory_space=pltpu.VMEM)] * 6,
        out_specs=pl.BlockSpec(memory_space=pltpu.VMEM),
        scratch_shapes=[
            pltpu.VMEM((2, 2, block, forcing, dofs), green.dtype),
            pltpu.SemaphoreType.DMA((2,)),
            pltpu.VMEM((2, wave_count, 8, dofs), jnp.float32),
            pltpu.VMEM((modes, dofs), jnp.float32),
            pltpu.VMEM((n_dof - 1, modes, dofs), jnp.float32),
            pltpu.VMEM((n_dof - 1, own, dofs), coupling.dtype),
            pltpu.VMEM((n_wave, pad, own), jnp.float32),
            pltpu.VMEM((n_wave - 1, pad, own), jnp.float32),
            pltpu.SemaphoreType.DMA((2, n_dof - 1)),
            pltpu.SemaphoreType.DMA((2, n_dof - 1)),
            pltpu.SemaphoreType.DMA((n_wave - 1,)),
            pltpu.SemaphoreType.DMA((n_wave - 1,)),
        ],
        compiler_params=pltpu.CompilerParams(collective_id=0, has_side_effects=True),
    )(green, lhs, coupling, rows_t, counts_row, pos_t, load_t)


def body(green, rough, axle_pos, axle_load, rows, counts, coupling):
    wave_count = green.shape[1]
    case_count = axle_pos.shape[0]
    building_count = rows.shape[0]
    slot_count = rows.shape[1]
    dof_size = lax.axis_size("dof")
    wave_size = lax.axis_size("wave")
    own_buildings = building_count // dof_size

    re_hi, re_lo = split_bf16(rough[0])
    im_hi, im_lo = split_bf16(rough[1])
    zero = jnp.zeros_like(re_hi)
    lhs = jnp.stack([re_hi, re_lo, im_hi, im_lo, zero, zero, zero, zero], axis=1)
    return exchange(green, lhs, coupling, rows.T, counts.reshape(1, -1), axle_pos.T, axle_load.T).T


def solution(mesh):
    in_specs = (
        P(None, "wave", None, "dof"),
        P(None, "wave", None),
        P(),
        P(),
        P(),
        P(),
        P(None, "dof"),
    )
    out_specs = P("dof", "wave")
    return jax.shard_map(body, mesh=mesh, in_specs=in_specs, out_specs=out_specs, check_vma=False)
```

```python
import math

import jax
import jax.numpy as jnp
from jax import lax
from jax.experimental import pallas as pl
from jax.experimental.pallas import tpu as pltpu
from jax.sharding import PartitionSpec as P

K = 2048


def split_bf16(x):
    hi = x.astype(jnp.bfloat16)
    lo = (x - hi.astype(jnp.float32)).astype(jnp.bfloat16)
    return hi, lo


def exchange(vt, vt_link, rows_t, counts_row, pos_t, load_t, wave_count):
    n_dof = lax.axis_size("dof")
    n_wave = lax.axis_size("wave")
    modes = vt.shape[0]
    own = vt.shape[1] // n_dof
    slots, cases = rows_t.shape[0], pos_t.shape[1]
    axles = pos_t.shape[0]
    per_wave = cases // n_wave
    pad = 8
    mesh_id = pl.DeviceIdType.MESH
    step = 2.0 * math.pi / K
    scale = 1.0 / math.sqrt(K)
    norm_axle = 1.0 / math.sqrt(axles)
    group = 8
    groups = wave_count // group

    def turns(m_first, station):
        v_col = lax.broadcasted_iota(jnp.int32, (group, 1), 0)
        coarse = (((m_first + group * v_col) * station) & (K - 1)).astype(jnp.float32) * step
        fine = ((v_col * station) & (K - 1)).astype(jnp.float32) * step
        c_coarse, s_coarse = jnp.cos(coarse), jnp.sin(coarse)
        c_fine, s_fine = jnp.cos(fine), jnp.sin(fine)
        blocks = []
        for u in range(groups):
            cu = c_coarse[u : u + 1, :]
            su = s_coarse[u : u + 1, :]
            blocks.append((cu * c_fine - su * s_fine, su * c_fine + cu * s_fine))
        return blocks

    def kernel(vt_ref, link_ref, rows_ref, counts_ref, pos_ref, load_ref, out_ref,
               recv_v, send_r, recv_r, v_send, v_recv, r_send, r_recv):
        me_d = lax.axis_index("dof")
        me_w = lax.axis_index("wave")
        barrier = pltpu.get_barrier_semaphore()
        for k in range(1, n_dof):
            pl.semaphore_signal(barrier, inc=1, device_id={"dof": lax.rem(me_d + k, n_dof)}, device_id_type=mesh_id)
        for k in range(1, n_wave):
            pl.semaphore_signal(barrier, inc=1, device_id={"wave": lax.rem(me_w + k, n_wave)}, device_id_type=mesh_id)

        pl.semaphore_wait(barrier, n_dof - 1 + n_wave - 1)
        v_copies = []
        for k in range(1, n_dof):
            peer = lax.rem(me_d + k, n_dof)
            copy = pltpu.make_async_remote_copy(
                src_ref=link_ref.at[:, pl.ds(pl.multiple_of(peer * own, own), own)],
                dst_ref=recv_v.at[k - 1],
                send_sem=v_send.at[k - 1],
                recv_sem=v_recv.at[k - 1],
                device_id={"dof": peer},
                device_id_type=mesh_id,
            )
            copy.start()
            v_copies.append(copy)

        m_first = me_w * wave_count
        mine = pl.ds(pl.multiple_of(me_d * own, own), own)
        count = counts_ref[:, mine]
        w_re = [jnp.zeros((group, own), jnp.float32) for _ in range(groups)]
        w_im = [jnp.zeros((group, own), jnp.float32) for _ in range(groups)]
        for s in range(slots):
            station = rows_ref[s : s + 1, mine]
            used = jnp.where(count > s, 1.0, 0.0)
            for u, (c, sn) in enumerate(turns(m_first, station)):
                t_re = (c * scale).astype(jnp.bfloat16).astype(jnp.float32)
                t_im = (-sn * scale).astype(jnp.bfloat16).astype(jnp.float32)
                w_re[u] = w_re[u] + used * t_re
                w_im[u] = w_im[u] + used * t_im
        w_re = jnp.concatenate(w_re, axis=0)
        w_im = jnp.concatenate(w_im, axis=0)

        p_re = [jnp.zeros((group, cases), jnp.float32) for _ in range(groups)]
        p_im = [jnp.zeros((group, cases), jnp.float32) for _ in range(groups)]
        for a in range(axles):
            load = load_ref[a : a + 1, :]
            for u, (c, sn) in enumerate(turns(m_first, pos_ref[a : a + 1, :])):
                p_re[u] = p_re[u] + load * c
                p_im[u] = p_im[u] + load * sn
        p_re = jnp.concatenate(p_re, axis=0)
        p_im = jnp.concatenate(p_im, axis=0)
        phase = jnp.concatenate([p_re * norm_axle, -p_im * norm_axle], axis=0)

        row = lax.broadcasted_iota(jnp.int32, (n_wave * pad, cases), 0)
        col = lax.broadcasted_iota(jnp.int32, (n_wave * pad, cases), 1)
        spread = jnp.where(
            (col == (row // pad) * per_wave + row % pad) & (row % pad < per_wave), 1.0, 0.0
        ).astype(jnp.bfloat16)
        ph_hi, ph_lo = split_bf16(phase)
        dims = (((1,), (1,)), ((), ()))
        pt_hi = lax.dot_general(spread, ph_hi, dims, preferred_element_type=jnp.float32).astype(jnp.bfloat16)
        pt_lo = lax.dot_general(spread, ph_lo, dims, preferred_element_type=jnp.float32).astype(jnp.bfloat16)

        for copy in v_copies:
            copy.wait()
        total = vt_ref[:, pl.ds(pl.multiple_of(me_d * own, own), own)]
        for k in range(n_dof - 1):
            total = total + recv_v[k].astype(jnp.float32)
        v_re = total[0:wave_count]
        v_im = total[wave_count : 2 * wave_count]
        ab = jnp.concatenate([w_re * v_re + w_im * v_im, w_im * v_re - w_re * v_im], axis=0)
        ab_hi, ab_lo = split_bf16(ab)
        r_pad = (
            jnp.dot(pt_hi, ab_hi, preferred_element_type=jnp.float32)
            + jnp.dot(pt_hi, ab_lo, preferred_element_type=jnp.float32)
            + jnp.dot(pt_lo, ab_hi, preferred_element_type=jnp.float32)
        )
        for p in range(n_wave):
            send_r[p] = r_pad[p * pad : (p + 1) * pad]
        result = send_r[me_w]

        r_copies = []
        for k in range(1, n_wave):
            peer = lax.rem(me_w + k, n_wave)
            copy = pltpu.make_async_remote_copy(
                src_ref=send_r.at[peer, 0:per_wave],
                dst_ref=recv_r.at[k - 1, 0:per_wave],
                send_sem=r_send.at[k - 1],
                recv_sem=r_recv.at[k - 1],
                device_id={"wave": peer},
                device_id_type=mesh_id,
            )
            copy.start()
            r_copies.append(copy)
        for copy in r_copies:
            copy.wait()
        result = result[0:per_wave]
        for k in range(n_wave - 1):
            result = result + recv_r[k, 0:per_wave]
        out_ref[...] = result / count.astype(jnp.float32)

    return pl.pallas_call(
        kernel,
        out_shape=jax.ShapeDtypeStruct((per_wave, own), jnp.float32),
        in_specs=[pl.BlockSpec(memory_space=pltpu.VMEM)] * 6,
        out_specs=pl.BlockSpec(memory_space=pltpu.VMEM),
        scratch_shapes=[
            pltpu.VMEM((n_dof - 1, modes, own), vt_link.dtype),
            pltpu.VMEM((n_wave, pad, own), jnp.float32),
            pltpu.VMEM((n_wave - 1, pad, own), jnp.float32),
            pltpu.SemaphoreType.DMA((n_dof - 1,)),
            pltpu.SemaphoreType.DMA((n_dof - 1,)),
            pltpu.SemaphoreType.DMA((n_wave - 1,)),
            pltpu.SemaphoreType.DMA((n_wave - 1,)),
        ],
        compiler_params=pltpu.CompilerParams(collective_id=0, has_side_effects=True),
    )(vt, vt_link, rows_t, counts_row, pos_t, load_t)


def body(green, rough, axle_pos, axle_load, rows, counts, coupling):
    wave_count = green.shape[1]
    case_count = axle_pos.shape[0]
    building_count = rows.shape[0]
    slot_count = rows.shape[1]
    dof_size = lax.axis_size("dof")
    wave_size = lax.axis_size("wave")
    own_buildings = building_count // dof_size

    re_hi, re_lo = split_bf16(rough[0])
    im_hi, im_lo = split_bf16(rough[1])
    lhs = jnp.stack([re_hi, re_lo, im_hi, im_lo], axis=1)
    prod = jnp.einsum("mkj,gmji->gmki", lhs, green, preferred_element_type=jnp.float32)
    gre_rre = prod[0, :, 0] + prod[0, :, 1]
    gre_rim = prod[0, :, 2] + prod[0, :, 3]
    gim_rre = prod[1, :, 0] + prod[1, :, 1]
    gim_rim = prod[1, :, 2] + prod[1, :, 3]
    h_cat = jnp.concatenate([gre_rre - gim_rim, gre_rim + gim_rre], axis=0)

    vt_part = lax.dot_general(
        h_cat, coupling, (((1,), (1,)), ((), ())),
        precision=lax.Precision.HIGHEST, preferred_element_type=jnp.float32,
    )
    return exchange(vt_part, vt_part.astype(jnp.bfloat16), rows.T, counts.reshape(1, -1), axle_pos.T, axle_load.T, wave_count).T


def solution(mesh):
    in_specs = (
        P(None, "wave", None, "dof"),
        P(None, "wave", None),
        P(),
        P(),
        P(),
        P(),
        P(None, "dof"),
    )
    out_specs = P("dof", "wave")
    return jax.shard_map(body, mesh=mesh, in_specs=in_specs, out_specs=out_specs, check_vma=False)
```

```python
import math

import jax
import jax.numpy as jnp
from jax import lax
from jax.experimental import pallas as pl
from jax.experimental.pallas import tpu as pltpu
from jax.sharding import PartitionSpec as P

K = 2048


def split_bf16(x):
    hi = x.astype(jnp.bfloat16)
    lo = (x - hi.astype(jnp.float32)).astype(jnp.bfloat16)
    return hi, lo


def exchange(h_cat, coupling, rows_t, counts_row, pos_t, load_t, wave_count):
    n_dof = lax.axis_size("dof")
    n_wave = lax.axis_size("wave")
    modes = h_cat.shape[0]
    own = coupling.shape[0] // n_dof
    slots, cases = rows_t.shape[0], pos_t.shape[1]
    axles = pos_t.shape[0]
    per_wave = cases // n_wave
    pad = 8
    mesh_id = pl.DeviceIdType.MESH
    step = 2.0 * math.pi / K
    scale = 1.0 / math.sqrt(K)
    norm_axle = 1.0 / math.sqrt(axles)
    group = 8
    groups = wave_count // group

    def turns(m_first, station):
        v_col = lax.broadcasted_iota(jnp.int32, (group, 1), 0)
        coarse = (((m_first + group * v_col) * station) & (K - 1)).astype(jnp.float32) * step
        fine = ((v_col * station) & (K - 1)).astype(jnp.float32) * step
        c_coarse, s_coarse = jnp.cos(coarse), jnp.sin(coarse)
        c_fine, s_fine = jnp.cos(fine), jnp.sin(fine)
        blocks = []
        for u in range(groups):
            cu = c_coarse[u : u + 1, :]
            su = s_coarse[u : u + 1, :]
            blocks.append((cu * c_fine - su * s_fine, su * c_fine + cu * s_fine))
        return blocks

    def kernel(h_ref, cpl_ref, rows_ref, counts_ref, pos_ref, load_ref, out_ref,
               link_ref, recv_v, send_r, recv_r, v_send, v_recv, r_send, r_recv):
        me_d = lax.axis_index("dof")
        me_w = lax.axis_index("wave")
        barrier = pltpu.get_barrier_semaphore()
        for k in range(1, n_dof):
            pl.semaphore_signal(barrier, inc=1, device_id={"dof": lax.rem(me_d + k, n_dof)}, device_id_type=mesh_id)
        for k in range(1, n_wave):
            pl.semaphore_signal(barrier, inc=1, device_id={"wave": lax.rem(me_w + k, n_wave)}, device_id_type=mesh_id)

        h_hi, h_lo = split_bf16(h_ref[...])
        dims_t = (((1,), (1,)), ((), ()))

        def v_of(c):
            return (lax.dot_general(h_hi, c, dims_t, preferred_element_type=jnp.float32)
                    + lax.dot_general(h_lo, c, dims_t, preferred_element_type=jnp.float32))

        link_ref[...] = v_of(cpl_ref[...]).astype(link_ref.dtype)
        mine = pl.ds(pl.multiple_of(me_d * own, own), own)
        total = v_of(cpl_ref[mine, :])
        pl.semaphore_wait(barrier, n_dof - 1 + n_wave - 1)
        v_copies = []
        for k in range(1, n_dof):
            peer = lax.rem(me_d + k, n_dof)
            copy = pltpu.make_async_remote_copy(
                src_ref=link_ref.at[:, pl.ds(pl.multiple_of(peer * own, own), own)],
                dst_ref=recv_v.at[k - 1],
                send_sem=v_send.at[k - 1],
                recv_sem=v_recv.at[k - 1],
                device_id={"dof": peer},
                device_id_type=mesh_id,
            )
            copy.start()
            v_copies.append(copy)

        m_first = me_w * wave_count
        count = counts_ref[:, mine]
        w_re = [jnp.zeros((group, own), jnp.float32) for _ in range(groups)]
        w_im = [jnp.zeros((group, own), jnp.float32) for _ in range(groups)]
        for s in range(slots):
            station = rows_ref[s : s + 1, mine]
            used = jnp.where(count > s, 1.0, 0.0)
            for u, (c, sn) in enumerate(turns(m_first, station)):
                t_re = (c * scale).astype(jnp.bfloat16).astype(jnp.float32)
                t_im = (-sn * scale).astype(jnp.bfloat16).astype(jnp.float32)
                w_re[u] = w_re[u] + used * t_re
                w_im[u] = w_im[u] + used * t_im
        w_re = jnp.concatenate(w_re, axis=0)
        w_im = jnp.concatenate(w_im, axis=0)

        p_re = [jnp.zeros((group, cases), jnp.float32) for _ in range(groups)]
        p_im = [jnp.zeros((group, cases), jnp.float32) for _ in range(groups)]
        for a in range(axles):
            load = load_ref[a : a + 1, :]
            for u, (c, sn) in enumerate(turns(m_first, pos_ref[a : a + 1, :])):
                p_re[u] = p_re[u] + load * c
                p_im[u] = p_im[u] + load * sn
        p_re = jnp.concatenate(p_re, axis=0)
        p_im = jnp.concatenate(p_im, axis=0)
        phase = jnp.concatenate([p_re * norm_axle, -p_im * norm_axle], axis=0)

        row = lax.broadcasted_iota(jnp.int32, (n_wave * pad, cases), 0)
        col = lax.broadcasted_iota(jnp.int32, (n_wave * pad, cases), 1)
        spread = jnp.where(
            (col == (row // pad) * per_wave + row % pad) & (row % pad < per_wave), 1.0, 0.0
        ).astype(jnp.bfloat16)
        ph_hi, ph_lo = split_bf16(phase)
        dims = (((1,), (1,)), ((), ()))
        pt_hi = lax.dot_general(spread, ph_hi, dims, preferred_element_type=jnp.float32).astype(jnp.bfloat16)
        pt_lo = lax.dot_general(spread, ph_lo, dims, preferred_element_type=jnp.float32).astype(jnp.bfloat16)

        for copy in v_copies:
            copy.wait()
        for k in range(n_dof - 1):
            total = total + recv_v[k].astype(jnp.float32)
        v_re = total[0:wave_count]
        v_im = total[wave_count : 2 * wave_count]
        ab = jnp.concatenate([w_re * v_re + w_im * v_im, w_im * v_re - w_re * v_im], axis=0)
        ab_hi, ab_lo = split_bf16(ab)
        r_pad = (
            jnp.dot(pt_hi, ab_hi, preferred_element_type=jnp.float32)
            + jnp.dot(pt_hi, ab_lo, preferred_element_type=jnp.float32)
            + jnp.dot(pt_lo, ab_hi, preferred_element_type=jnp.float32)
        )
        for p in range(n_wave):
            send_r[p] = r_pad[p * pad : (p + 1) * pad]
        result = send_r[me_w]

        r_copies = []
        for k in range(1, n_wave):
            peer = lax.rem(me_w + k, n_wave)
            copy = pltpu.make_async_remote_copy(
                src_ref=send_r.at[peer, 0:per_wave],
                dst_ref=recv_r.at[k - 1, 0:per_wave],
                send_sem=r_send.at[k - 1],
                recv_sem=r_recv.at[k - 1],
                device_id={"wave": peer},
                device_id_type=mesh_id,
            )
            copy.start()
            r_copies.append(copy)
        for copy in r_copies:
            copy.wait()
        result = result[0:per_wave]
        for k in range(n_wave - 1):
            result = result + recv_r[k, 0:per_wave]
        out_ref[...] = result / count.astype(jnp.float32)

    return pl.pallas_call(
        kernel,
        out_shape=jax.ShapeDtypeStruct((per_wave, own), jnp.float32),
        in_specs=[pl.BlockSpec(memory_space=pltpu.VMEM)] * 6,
        out_specs=pl.BlockSpec(memory_space=pltpu.VMEM),
        scratch_shapes=[
            pltpu.VMEM((modes, n_dof * own), jnp.bfloat16),
            pltpu.VMEM((n_dof - 1, modes, own), jnp.bfloat16),
            pltpu.VMEM((n_wave, pad, own), jnp.float32),
            pltpu.VMEM((n_wave - 1, pad, own), jnp.float32),
            pltpu.SemaphoreType.DMA((n_dof - 1,)),
            pltpu.SemaphoreType.DMA((n_dof - 1,)),
            pltpu.SemaphoreType.DMA((n_wave - 1,)),
            pltpu.SemaphoreType.DMA((n_wave - 1,)),
        ],
        compiler_params=pltpu.CompilerParams(collective_id=0, has_side_effects=True),
    )(h_cat, coupling, rows_t, counts_row, pos_t, load_t)


def body(green, rough, axle_pos, axle_load, rows, counts, coupling):
    wave_count = green.shape[1]
    case_count = axle_pos.shape[0]
    building_count = rows.shape[0]
    slot_count = rows.shape[1]
    dof_size = lax.axis_size("dof")
    wave_size = lax.axis_size("wave")
    own_buildings = building_count // dof_size

    re_hi, re_lo = split_bf16(rough[0])
    im_hi, im_lo = split_bf16(rough[1])
    lhs = jnp.stack([re_hi, re_lo, im_hi, im_lo], axis=1)
    prod = jnp.einsum("mkj,gmji->gmki", lhs, green, preferred_element_type=jnp.float32)
    gre_rre = prod[0, :, 0] + prod[0, :, 1]
    gre_rim = prod[0, :, 2] + prod[0, :, 3]
    gim_rre = prod[1, :, 0] + prod[1, :, 1]
    gim_rim = prod[1, :, 2] + prod[1, :, 3]
    h_cat = jnp.concatenate([gre_rre - gim_rim, gre_rim + gim_rre], axis=0)

    return exchange(h_cat, coupling, rows.T, counts.reshape(1, -1), axle_pos.T, axle_load.T, wave_count).T


def solution(mesh):
    in_specs = (
        P(None, "wave", None, "dof"),
        P(None, "wave", None),
        P(),
        P(),
        P(),
        P(),
        P(None, "dof"),
    )
    out_specs = P("dof", "wave")
    return jax.shard_map(body, mesh=mesh, in_specs=in_specs, out_specs=out_specs, check_vma=False)
```

```python
import math

import jax
import jax.numpy as jnp
from jax import lax
from jax.experimental import pallas as pl
from jax.experimental.pallas import tpu as pltpu
from jax.sharding import PartitionSpec as P

K = 2048


def split_bf16(x):
    hi = x.astype(jnp.bfloat16)
    lo = (x - hi.astype(jnp.float32)).astype(jnp.bfloat16)
    return hi, lo


def exchange(h_cat, coupling, rows_t, counts_row, pos_t, load_t, wave_count):
    n_dof = lax.axis_size("dof")
    n_wave = lax.axis_size("wave")
    modes = h_cat.shape[0]
    own = coupling.shape[0] // n_dof
    slots, cases = rows_t.shape[0], pos_t.shape[1]
    axles = pos_t.shape[0]
    per_wave = cases // n_wave
    pad = 8
    mesh_id = pl.DeviceIdType.MESH
    step = 2.0 * math.pi / K
    scale = 1.0 / math.sqrt(K)
    norm_axle = 1.0 / math.sqrt(axles)
    group = 8
    groups = wave_count // group

    def turns(m_first, station):
        v_col = lax.broadcasted_iota(jnp.int32, (group, 1), 0)
        coarse = (((m_first + group * v_col) * station) & (K - 1)).astype(jnp.float32) * step
        fine = ((v_col * station) & (K - 1)).astype(jnp.float32) * step
        c_coarse, s_coarse = jnp.cos(coarse), jnp.sin(coarse)
        c_fine, s_fine = jnp.cos(fine), jnp.sin(fine)
        blocks = []
        for u in range(groups):
            cu = c_coarse[u : u + 1, :]
            su = s_coarse[u : u + 1, :]
            blocks.append((cu * c_fine - su * s_fine, su * c_fine + cu * s_fine))
        return blocks

    def kernel(h_ref, cpl_ref, rows_ref, counts_ref, pos_ref, load_ref, out_ref,
               link_ref, recv_v, send_r, recv_r, v_send, v_recv, r_send, r_recv):
        me_d = lax.axis_index("dof")
        me_w = lax.axis_index("wave")
        barrier = pltpu.get_barrier_semaphore()
        for k in range(1, n_dof):
            pl.semaphore_signal(barrier, inc=1, device_id={"dof": lax.rem(me_d + k, n_dof)}, device_id_type=mesh_id)
        for k in range(1, n_wave):
            pl.semaphore_signal(barrier, inc=1, device_id={"wave": lax.rem(me_w + k, n_wave)}, device_id_type=mesh_id)

        h_hi, h_lo = split_bf16(h_ref[...])
        dims_t = (((1,), (1,)), ((), ()))

        def v_of(c):
            return (lax.dot_general(h_hi, c, dims_t, preferred_element_type=jnp.float32)
                    + lax.dot_general(h_lo, c, dims_t, preferred_element_type=jnp.float32))

        link_ref[...] = v_of(cpl_ref[...]).astype(link_ref.dtype)
        mine = pl.ds(pl.multiple_of(me_d * own, own), own)
        total = v_of(cpl_ref[mine, :])
        pl.semaphore_wait(barrier, n_dof - 1 + n_wave - 1)
        v_copies = []
        for k in range(1, n_dof):
            peer = lax.rem(me_d + k, n_dof)
            copy = pltpu.make_async_remote_copy(
                src_ref=link_ref.at[:, pl.ds(pl.multiple_of(peer * own, own), own)],
                dst_ref=recv_v.at[k - 1],
                send_sem=v_send.at[k - 1],
                recv_sem=v_recv.at[k - 1],
                device_id={"dof": peer},
                device_id_type=mesh_id,
            )
            copy.start()
            v_copies.append(copy)

        m_first = me_w * wave_count
        count = counts_ref[:, mine]
        w_re = [jnp.zeros((group, own), jnp.float32) for _ in range(groups)]
        w_im = [jnp.zeros((group, own), jnp.float32) for _ in range(groups)]
        for s in range(slots):
            station = rows_ref[s : s + 1, mine]
            used = jnp.where(count > s, 1.0, 0.0)
            for u, (c, sn) in enumerate(turns(m_first, station)):
                t_re = (c * scale).astype(jnp.bfloat16).astype(jnp.float32)
                t_im = (-sn * scale).astype(jnp.bfloat16).astype(jnp.float32)
                w_re[u] = w_re[u] + used * t_re
                w_im[u] = w_im[u] + used * t_im
        w_re = jnp.concatenate(w_re, axis=0)
        w_im = jnp.concatenate(w_im, axis=0)

        p_re = [jnp.zeros((group, cases), jnp.float32) for _ in range(groups)]
        p_im = [jnp.zeros((group, cases), jnp.float32) for _ in range(groups)]
        for a in range(axles):
            load = load_ref[a : a + 1, :]
            for u, (c, sn) in enumerate(turns(m_first, pos_ref[a : a + 1, :])):
                p_re[u] = p_re[u] + load * c
                p_im[u] = p_im[u] + load * sn
        p_re = jnp.concatenate(p_re, axis=0)
        p_im = jnp.concatenate(p_im, axis=0)
        phase = jnp.concatenate([p_re * norm_axle, -p_im * norm_axle], axis=0)

        row = lax.broadcasted_iota(jnp.int32, (n_wave * pad, cases), 0)
        col = lax.broadcasted_iota(jnp.int32, (n_wave * pad, cases), 1)
        spread = jnp.where(
            (col == (row // pad) * per_wave + row % pad) & (row % pad < per_wave), 1.0, 0.0
        ).astype(jnp.bfloat16)
        ph_hi, ph_lo = split_bf16(phase)
        dims = (((1,), (1,)), ((), ()))
        pt_hi = lax.dot_general(spread, ph_hi, dims, preferred_element_type=jnp.float32).astype(jnp.bfloat16)
        pt_lo = lax.dot_general(spread, ph_lo, dims, preferred_element_type=jnp.float32).astype(jnp.bfloat16)

        for copy in v_copies:
            copy.wait()
        for k in range(n_dof - 1):
            total = total + recv_v[k].astype(jnp.float32)
        v_re = total[0:wave_count]
        v_im = total[wave_count : 2 * wave_count]
        ab = jnp.concatenate([w_re * v_re + w_im * v_im, w_im * v_re - w_re * v_im], axis=0)
        ab_hi, ab_lo = split_bf16(ab)
        r_pad = (
            jnp.dot(pt_hi, ab_hi, preferred_element_type=jnp.float32)
            + jnp.dot(pt_hi, ab_lo, preferred_element_type=jnp.float32)
            + jnp.dot(pt_lo, ab_hi, preferred_element_type=jnp.float32)
        )
        for p in range(n_wave):
            send_r[p] = r_pad[p * pad : (p + 1) * pad]
        result = send_r[me_w]

        r_copies = []
        for k in range(1, n_wave):
            peer = lax.rem(me_w + k, n_wave)
            copy = pltpu.make_async_remote_copy(
                src_ref=send_r.at[peer, 0:per_wave],
                dst_ref=recv_r.at[k - 1, 0:per_wave],
                send_sem=r_send.at[k - 1],
                recv_sem=r_recv.at[k - 1],
                device_id={"wave": peer},
                device_id_type=mesh_id,
            )
            copy.start()
            r_copies.append(copy)
        for copy in r_copies:
            copy.wait()
        result = result[0:per_wave]
        for k in range(n_wave - 1):
            result = result + recv_r[k, 0:per_wave]
        out_ref[...] = result / count.astype(jnp.float32)

    return pl.pallas_call(
        kernel,
        out_shape=jax.ShapeDtypeStruct((per_wave, own), jnp.float32),
        in_specs=[pl.BlockSpec(memory_space=pltpu.VMEM)] * 6,
        out_specs=pl.BlockSpec(memory_space=pltpu.VMEM),
        scratch_shapes=[
            pltpu.VMEM((modes, n_dof * own), jnp.bfloat16),
            pltpu.VMEM((n_dof - 1, modes, own), jnp.bfloat16),
            pltpu.VMEM((n_wave, pad, own), jnp.float32),
            pltpu.VMEM((n_wave - 1, pad, own), jnp.float32),
            pltpu.SemaphoreType.DMA((n_dof - 1,)),
            pltpu.SemaphoreType.DMA((n_dof - 1,)),
            pltpu.SemaphoreType.DMA((n_wave - 1,)),
            pltpu.SemaphoreType.DMA((n_wave - 1,)),
        ],
        compiler_params=pltpu.CompilerParams(collective_id=0, has_side_effects=True),
    )(h_cat, coupling, rows_t, counts_row, pos_t, load_t)


def body(green, rough, axle_pos, axle_load, rows, counts, coupling):
    wave_count = green.shape[1]
    case_count = axle_pos.shape[0]
    building_count = rows.shape[0]
    slot_count = rows.shape[1]
    dof_size = lax.axis_size("dof")
    wave_size = lax.axis_size("wave")
    own_buildings = building_count // dof_size

    lhs = jnp.transpose(rough, (1, 0, 2))
    prod = jnp.einsum("mkj,gmji->gmki", lhs, green.astype(jnp.float32),
                      precision=lax.Precision.HIGH, preferred_element_type=jnp.float32)
    gre_rre = prod[0, :, 0]
    gre_rim = prod[0, :, 1]
    gim_rre = prod[1, :, 0]
    gim_rim = prod[1, :, 1]
    h_cat = jnp.concatenate([gre_rre - gim_rim, gre_rim + gim_rre], axis=0)

    return exchange(h_cat, coupling, rows.T, counts.reshape(1, -1), axle_pos.T, axle_load.T, wave_count).T


def solution(mesh):
    in_specs = (
        P(None, "wave", None, "dof"),
        P(None, "wave", None),
        P(),
        P(),
        P(),
        P(),
        P(None, "dof"),
    )
    out_specs = P("dof", "wave")
    return jax.shard_map(body, mesh=mesh, in_specs=in_specs, out_specs=out_specs, check_vma=False)
```

```python
import math

import jax
import jax.numpy as jnp
from jax import lax
from jax.experimental import pallas as pl
from jax.experimental.pallas import tpu as pltpu
from jax.sharding import PartitionSpec as P

K = 2048


def split_bf16(x):
    hi = x.astype(jnp.bfloat16)
    lo = (x - hi.astype(jnp.float32)).astype(jnp.bfloat16)
    return hi, lo


def exchange(h_cat, coupling, rows_t, counts_row, pos_t, load_t, wave_count):
    n_dof = lax.axis_size("dof")
    n_wave = lax.axis_size("wave")
    modes = h_cat.shape[0]
    own = coupling.shape[0] // n_dof
    slots, cases = rows_t.shape[0], pos_t.shape[1]
    axles = pos_t.shape[0]
    per_wave = cases // n_wave
    pad = 8
    mesh_id = pl.DeviceIdType.MESH
    step = 2.0 * math.pi / K
    scale = 1.0 / math.sqrt(K)
    norm_axle = 1.0 / math.sqrt(axles)
    group = 8
    groups = wave_count // group

    def turns(m_first, station):
        v_col = lax.broadcasted_iota(jnp.int32, (group, 1), 0)
        coarse = (((m_first + group * v_col) * station) & (K - 1)).astype(jnp.float32) * step
        fine = ((v_col * station) & (K - 1)).astype(jnp.float32) * step
        c_coarse, s_coarse = jnp.cos(coarse), jnp.sin(coarse)
        c_fine, s_fine = jnp.cos(fine), jnp.sin(fine)
        blocks = []
        for u in range(groups):
            cu = c_coarse[u : u + 1, :]
            su = s_coarse[u : u + 1, :]
            blocks.append((cu * c_fine - su * s_fine, su * c_fine + cu * s_fine))
        return blocks

    def kernel(h_ref, cpl_ref, rows_ref, counts_ref, pos_ref, load_ref, out_ref,
               link_ref, recv_v, send_r, recv_r, v_send, v_recv, r_send, r_recv):
        me_d = lax.axis_index("dof")
        me_w = lax.axis_index("wave")
        barrier = pltpu.get_barrier_semaphore()
        for k in range(1, n_dof):
            pl.semaphore_signal(barrier, inc=1, device_id={"dof": lax.rem(me_d + k, n_dof)}, device_id_type=mesh_id)
        for k in range(1, n_wave):
            pl.semaphore_signal(barrier, inc=1, device_id={"wave": lax.rem(me_w + k, n_wave)}, device_id_type=mesh_id)

        h_hi, h_lo = split_bf16(h_ref[...])
        dims_t = (((1,), (1,)), ((), ()))

        def v_of(c):
            return (lax.dot_general(h_hi, c, dims_t, preferred_element_type=jnp.float32)
                    + lax.dot_general(h_lo, c, dims_t, preferred_element_type=jnp.float32))

        link_ref[...] = v_of(cpl_ref[...]).astype(link_ref.dtype)
        mine = pl.ds(pl.multiple_of(me_d * own, own), own)
        total = v_of(cpl_ref[mine, :])
        pl.semaphore_wait(barrier, n_dof - 1 + n_wave - 1)
        v_copies = []
        for k in range(1, n_dof):
            peer = lax.rem(me_d + k, n_dof)
            copy = pltpu.make_async_remote_copy(
                src_ref=link_ref.at[:, pl.ds(pl.multiple_of(peer * own, own), own)],
                dst_ref=recv_v.at[k - 1],
                send_sem=v_send.at[k - 1],
                recv_sem=v_recv.at[k - 1],
                device_id={"dof": peer},
                device_id_type=mesh_id,
            )
            copy.start()
            v_copies.append(copy)

        m_first = me_w * wave_count
        count = counts_ref[:, mine]
        w_re = [jnp.zeros((group, own), jnp.float32) for _ in range(groups)]
        w_im = [jnp.zeros((group, own), jnp.float32) for _ in range(groups)]
        for s in range(slots):
            station = rows_ref[s : s + 1, mine]
            used = jnp.where(count > s, 1.0, 0.0)
            for u, (c, sn) in enumerate(turns(m_first, station)):
                t_re = (c * scale).astype(jnp.bfloat16).astype(jnp.float32)
                t_im = (-sn * scale).astype(jnp.bfloat16).astype(jnp.float32)
                w_re[u] = w_re[u] + used * t_re
                w_im[u] = w_im[u] + used * t_im
        w_re = jnp.concatenate(w_re, axis=0)
        w_im = jnp.concatenate(w_im, axis=0)

        p_re = [jnp.zeros((group, cases), jnp.float32) for _ in range(groups)]
        p_im = [jnp.zeros((group, cases), jnp.float32) for _ in range(groups)]
        for a in range(axles):
            load = load_ref[a : a + 1, :]
            for u, (c, sn) in enumerate(turns(m_first, pos_ref[a : a + 1, :])):
                p_re[u] = p_re[u] + load * c
                p_im[u] = p_im[u] + load * sn
        p_re = jnp.concatenate(p_re, axis=0)
        p_im = jnp.concatenate(p_im, axis=0)
        phase = jnp.concatenate([p_re * norm_axle, -p_im * norm_axle], axis=0)

        row = lax.broadcasted_iota(jnp.int32, (n_wave * pad, cases), 0)
        col = lax.broadcasted_iota(jnp.int32, (n_wave * pad, cases), 1)
        spread = jnp.where(
            (col == (row // pad) * per_wave + row % pad) & (row % pad < per_wave), 1.0, 0.0
        ).astype(jnp.bfloat16)
        ph_hi, ph_lo = split_bf16(phase)
        dims = (((1,), (1,)), ((), ()))
        pt_hi = lax.dot_general(spread, ph_hi, dims, preferred_element_type=jnp.float32).astype(jnp.bfloat16)
        pt_lo = lax.dot_general(spread, ph_lo, dims, preferred_element_type=jnp.float32).astype(jnp.bfloat16)

        for copy in v_copies:
            copy.wait()
        for k in range(n_dof - 1):
            total = total + recv_v[k].astype(jnp.float32)
        v_re = total[0:wave_count]
        v_im = total[wave_count : 2 * wave_count]
        ab = jnp.concatenate([w_re * v_re + w_im * v_im, w_im * v_re - w_re * v_im], axis=0)
        ab_hi, ab_lo = split_bf16(ab)
        r_pad = (
            jnp.dot(pt_hi, ab_hi, preferred_element_type=jnp.float32)
            + jnp.dot(pt_hi, ab_lo, preferred_element_type=jnp.float32)
            + jnp.dot(pt_lo, ab_hi, preferred_element_type=jnp.float32)
        )
        for p in range(n_wave):
            send_r[p] = r_pad[p * pad : (p + 1) * pad]
        result = send_r[me_w]

        r_copies = []
        for k in range(1, n_wave):
            peer = lax.rem(me_w + k, n_wave)
            copy = pltpu.make_async_remote_copy(
                src_ref=send_r.at[peer, 0:per_wave],
                dst_ref=recv_r.at[k - 1, 0:per_wave],
                send_sem=r_send.at[k - 1],
                recv_sem=r_recv.at[k - 1],
                device_id={"wave": peer},
                device_id_type=mesh_id,
            )
            copy.start()
            r_copies.append(copy)
        for copy in r_copies:
            copy.wait()
        result = result[0:per_wave]
        for k in range(n_wave - 1):
            result = result + recv_r[k, 0:per_wave]
        out_ref[...] = result / count.astype(jnp.float32)

    return pl.pallas_call(
        kernel,
        out_shape=jax.ShapeDtypeStruct((per_wave, own), jnp.float32),
        in_specs=[pl.BlockSpec(memory_space=pltpu.VMEM)] * 6,
        out_specs=pl.BlockSpec(memory_space=pltpu.VMEM),
        scratch_shapes=[
            pltpu.VMEM((modes, n_dof * own), jnp.bfloat16),
            pltpu.VMEM((n_dof - 1, modes, own), jnp.bfloat16),
            pltpu.VMEM((n_wave, pad, own), jnp.float32),
            pltpu.VMEM((n_wave - 1, pad, own), jnp.float32),
            pltpu.SemaphoreType.DMA((n_dof - 1,)),
            pltpu.SemaphoreType.DMA((n_dof - 1,)),
            pltpu.SemaphoreType.DMA((n_wave - 1,)),
            pltpu.SemaphoreType.DMA((n_wave - 1,)),
        ],
        compiler_params=pltpu.CompilerParams(collective_id=0, has_side_effects=True),
    )(h_cat, coupling, rows_t, counts_row, pos_t, load_t)


def body(green, rough, axle_pos, axle_load, rows, counts, coupling):
    wave_count = green.shape[1]
    case_count = axle_pos.shape[0]
    building_count = rows.shape[0]
    slot_count = rows.shape[1]
    dof_size = lax.axis_size("dof")
    wave_size = lax.axis_size("wave")
    own_buildings = building_count // dof_size

    prod = jnp.einsum("kmj,gmji->gmki", rough, green.astype(jnp.float32),
                      precision=lax.Precision.HIGH, preferred_element_type=jnp.float32)
    gre_rre = prod[0, :, 0]
    gre_rim = prod[0, :, 1]
    gim_rre = prod[1, :, 0]
    gim_rim = prod[1, :, 1]
    h_cat = jnp.concatenate([gre_rre - gim_rim, gre_rim + gim_rre], axis=0)

    return exchange(h_cat, coupling, rows.T, counts.reshape(1, -1), axle_pos.T, axle_load.T, wave_count).T


def solution(mesh):
    in_specs = (
        P(None, "wave", None, "dof"),
        P(None, "wave", None),
        P(),
        P(),
        P(),
        P(),
        P(None, "dof"),
    )
    out_specs = P("dof", "wave")
    return jax.shard_map(body, mesh=mesh, in_specs=in_specs, out_specs=out_specs, check_vma=False)
```
